32 devices in a mesh: seq: 4 (over y, core), shard: 8 (over z, x).
Axes of the slice: x: 2, y: 2, z: 4, core: 2. Of those that a mesh axis runs over, the one named last changes fastest.
Arguments:
- hidden_in: bfloat16 [8, 1024, 1024], P('shard', 'seq'), may hold values from -6 to 6
- norm_gain: float32 [1024], replicated, may hold values from 0.5 to 1.5
- in_weight: bfloat16 [1024, 4384], P('shard'), may hold values from -0.1875 to 0.1875
- conv_weight: float32 [4, 2304], replicated, may hold values from -3 to 3
- conv_bias: float32 [2304], replicated, may hold values from -0.5 to 0.5
- dt_bias: float32 [32], replicated, may hold values from -4 to -1
- a_log: float32 [32], replicated, may hold values from -6 to 1
- skip: float32 [32], replicated, may hold values from 0.5 to 1.5
- inner_gain: float32 [2048], replicated, may hold values from 0.5 to 1.5
- out_weight: bfloat16 [2048, 1024], P('shard'), may hold values from -0.125 to 0.125
- out_grad: float32 [8, 1024, 1024], P('shard', 'seq'), may hold values from -6 to 6
Outputs:
- block_out: float32 [8, 1024, 1024], P('shard', 'seq')
- input_grad: float32 [8, 1024, 1024], P('shard', 'seq')
- norm_gain_grad: float32 [1024], replicated
- in_weight_grad: float32 [1024, 4384], P('shard')
- conv_weight_grad: float32 [4, 2304], replicated
- conv_bias_grad: float32 [2304], replicated
- dt_bias_grad: float32 [32], replicated
- a_log_grad: float32 [32], replicated
- skip_grad: float32 [32], replicated
- inner_gain_grad: float32 [2048], replicated
- out_weight_grad: float32 [2048, 1024], P('shard')
The draws below stay inside these ranges and needn't reach their ends.
All inputs are finite; a program needn't handle non-finite values.
Results may differ from the reference program's by a relative error of at most 0.015.
Values may be sent and summed in bfloat16 or wider, within the bound.
No kernel may reach another device: no remote copies, remote signals or barrier semaphores. Data moves between devices by JAX's collectives and lax.ppermute only.
A program may use at most 128 MiB of HBM per device.

```python
import jax
import jax.numpy as jnp
from jax import lax

D = 1024
NH = 32
STATE = 128
CONV = 4
GROUP = 256
E = 2048
CD = 2304
F = 4384
LENGTH = 1024
SEQS = 8


def shard_levels(key, dims, cuts, least, top_value):
    level = 1.0
    for dim, blocks in cuts:
        steps = jax.random.uniform(jax.random.fold_in(jax.random.fold_in(key, 6), dim), (blocks,), jnp.float32, least / len(cuts), top_value / len(cuts))
        level = level * jnp.repeat(jnp.exp(steps), dims[dim] // blocks).reshape((-1,) + (1,) * (len(dims) - 1 - dim))
    return level


def gaussian(rng, extent, scale, bound, split=(), kind=jnp.bfloat16):
    loudness = shard_levels(rng, extent, split, -0.22, 0.18) if split else 1.0
    result = jax.random.normal(rng, extent, jnp.float32) * scale * loudness
    return jnp.minimum(jnp.maximum(result, -bound), bound).astype(kind)


def setup_inputs(seed: int = 0) -> dict:
    keys = jax.random.split(jax.random.key(seed), 12)
    return {
        "hidden_in": gaussian(keys[0], (SEQS, LENGTH, D), 1.0, 6.0, ((0, 8), (1, 4))),
        "norm_gain": jnp.clip(1.0 + 0.1 * jax.random.normal(keys[1], (D,), jnp.float32), 0.5, 1.5),
        "in_weight": gaussian(keys[2], (D, F), D ** -0.5, 0.1875, ((0, 8),)),
        "conv_weight": gaussian(keys[3], (CONV, CD), 0.5, 3.0, (), jnp.float32),
        "conv_bias": jnp.clip(jax.random.uniform(keys[4], (CD,), jnp.float32, -0.5, 0.5), -0.5, 0.5),
        "dt_bias": jnp.clip(jax.random.uniform(keys[5], (NH,), jnp.float32, -4.0, -1.0), -4.0, -1.0),
        "a_log": jnp.clip(jax.random.uniform(keys[6], (NH,), jnp.float32, -6.0, 1.0), -6.0, 1.0),
        "skip": jnp.clip(jax.random.uniform(keys[7], (NH,), jnp.float32, 0.5, 1.5), 0.5, 1.5),
        "inner_gain": jnp.clip(1.0 + 0.1 * jax.random.normal(keys[8], (E,), jnp.float32), 0.5, 1.5),
        "out_weight": gaussian(keys[9], (E, D), E ** -0.5, 0.125, ((0, 8),)),
        "out_grad": gaussian(keys[10], (SEQS, LENGTH, D), 1.0, 6.0, ((0, 8), (1, 4)), jnp.float32),
    }


norm_eps = 1e-05
highest = lax.Precision.HIGHEST

def section_one(conv_ext, dt_raw, conv_weight, conv_bias, dt_bias, a_log):
    rows = dt_raw.shape[0]
    width = conv_weight.shape[0]
    conv_out = conv_bias + conv_weight[0] * conv_ext[0:rows]
    for offset in range(1, width):
        conv_out = conv_out + conv_weight[offset] * conv_ext[offset:offset + rows]
    active = jax.nn.silu(conv_out)
    inner = conv_out.shape[1] - 2 * STATE
    x_heads = active[:, :inner]
    b_proj = active[:, inner:inner + STATE]
    c_proj = active[:, inner + STATE:]
    step_size = jax.nn.softplus(dt_raw + dt_bias)
    log_decay = -step_size * jnp.exp(a_log)
    return (x_heads, b_proj, c_proj, step_size, log_decay)

def ssd_groups(x_heads, b_proj, c_proj, step_size, log_decay, h_start):
    rows, heads = step_size.shape
    head_dim = x_heads.shape[1] // heads
    state_dim = b_proj.shape[1]
    blocks = rows // GROUP
    lower = jnp.arange(GROUP)[:, None] >= jnp.arange(GROUP)[None, :]
    mask = lower[None, :, :]

    def advance(state, pieces):
        x_blk, b_blk, c_blk, dt_blk, ld_blk = pieces
        cumul = jnp.cumsum(ld_blk, axis=0)
        cum_t = cumul.T
        spread = cum_t[:, :, None] - cum_t[:, None, :]
        kernel = jnp.where(mask, jnp.exp(jnp.where(mask, spread, 0.0)), 0.0)
        intersection = jnp.dot(c_blk, b_blk.T, precision=highest)
        kernel = kernel * intersection[None, :, :] * dt_blk.T[:, None, :]
        output = jnp.einsum('hts,shp->thp', kernel, x_blk, precision=highest)
        output = output + jnp.exp(cumul)[:, :, None] * jnp.einsum('hpn,tn->thp', state, c_blk, precision=highest)
        weight_tail = jnp.exp(cumul[-1][None, :] - cumul) * dt_blk
        fresh = jnp.einsum('sh,shp,sn->hpn', weight_tail, x_blk, b_blk, precision=highest)
        state = jnp.exp(cumul[-1])[:, None, None] * state + fresh
        return (state, output)
    pieces = (x_heads.reshape(blocks, GROUP, heads, head_dim), b_proj.reshape(blocks, GROUP, state_dim), c_proj.reshape(blocks, GROUP, state_dim), step_size.reshape(blocks, GROUP, heads), log_decay.reshape(blocks, GROUP, heads))
    h_end, outputs = lax.scan(advance, h_start, pieces)
    return (outputs.reshape(rows, heads * head_dim), h_end)

def section_three(ssd_out, x_heads, gate_z, skip, inner_gain):
    rows = ssd_out.shape[0]
    heads = skip.shape[0]
    mixed = ssd_out + (x_heads.reshape(rows, heads, -1) * skip[None, :, None]).reshape(rows, -1)
    gated_in = mixed * jax.nn.silu(gate_z)
    scale = lax.rsqrt(lax.optimization_barrier(jnp.mean(gated_in * gated_in, axis=-1, keepdims=True)) + norm_eps)
    return gated_in * scale * inner_gain

def reference(hidden_in, norm_gain, in_weight, conv_weight, conv_bias, dt_bias, a_log, skip, inner_gain, out_weight, out_grad):
    inner = inner_gain.shape[0]
    conv_dim = conv_bias.shape[0]
    width = conv_weight.shape[0]
    heads = dt_bias.shape[0]
    head_dim = inner // heads

    def one_sequence(totals, pieces):
        tokens, cotan = pieces
        tokens_f = tokens.astype(jnp.float32)
        rstat = lax.rsqrt(lax.optimization_barrier(jnp.mean(tokens_f * tokens_f, axis=-1, keepdims=True)) + norm_eps)
        normed = (tokens_f * rstat * norm_gain).astype(jnp.bfloat16)
        projected = jnp.dot(normed, in_weight, preferred_element_type=jnp.float32)
        gate_z = projected[:, :inner]
        conv_in = projected[:, inner:inner + conv_dim].astype(jnp.bfloat16)
        dt_raw = projected[:, inner + conv_dim:]
        conv_ext = jnp.concatenate([jnp.zeros((width - 1, conv_dim), jnp.float32), conv_in.astype(jnp.float32)], axis=0)
        firsts, back_one = jax.vjp(section_one, conv_ext, dt_raw, conv_weight, conv_bias, dt_bias, a_log)
        x_heads, b_proj, c_proj, step_size, log_decay = firsts
        h_zero = jnp.zeros((heads, head_dim, b_proj.shape[1]), jnp.float32)

        def scan_states(x_one, b_one, c_one, s_one, l_one):
            return ssd_groups(x_one, b_one, c_one, s_one, l_one, h_zero)
        (ssd_out, h_end), back_two = jax.vjp(scan_states, x_heads, b_proj, c_proj, step_size, log_decay)
        gated_pre, back_three = jax.vjp(section_three, ssd_out, x_heads, gate_z, skip, inner_gain)
        gated = gated_pre.astype(jnp.bfloat16)
        block = tokens_f + jnp.dot(gated, out_weight, preferred_element_type=jnp.float32)
        cot_b = cotan.astype(jnp.bfloat16)
        out_term = jnp.dot(gated.T, cot_b, preferred_element_type=jnp.float32)
        d_gated = jnp.dot(cot_b, out_weight.T, preferred_element_type=jnp.float32)
        d_ssd, d_x_three, d_gate, skip_term, gain_term = back_three(d_gated)
        d_x_two, d_b, d_c, d_step, d_log = back_two((d_ssd, jnp.zeros_like(h_end)))
        d_ext, d_dt_raw, convw_term, convb_term, dtb_term, alog_term = back_one((d_x_two + d_x_three, d_b, d_c, d_step, d_log))
        d_proj = jnp.concatenate([d_gate, d_ext[width - 1:], d_dt_raw], axis=1).astype(jnp.bfloat16)
        in_term = jnp.dot(normed.T, d_proj, preferred_element_type=jnp.float32)
        d_normed = jnp.dot(d_proj, in_weight.T, preferred_element_type=jnp.float32)
        norm_term = lax.optimization_barrier(jnp.sum(d_normed * tokens_f * rstat, axis=0))
        scaled = norm_gain * d_normed
        grad_in = cotan + rstat * scaled - tokens_f * rstat * rstat * rstat * lax.optimization_barrier(jnp.mean(scaled * tokens_f, axis=-1, keepdims=True))
        terms = (norm_term, in_term, convw_term, convb_term, dtb_term, alog_term, skip_term, gain_term, out_term)
        totals = tuple((total + term for total, term in zip(totals, terms)))
        return (totals, (block, grad_in))
    start = (jnp.zeros(norm_gain.shape, jnp.float32), jnp.zeros(in_weight.shape, jnp.float32), jnp.zeros(conv_weight.shape, jnp.float32), jnp.zeros(conv_bias.shape, jnp.float32), jnp.zeros(dt_bias.shape, jnp.float32), jnp.zeros(a_log.shape, jnp.float32), jnp.zeros(skip.shape, jnp.float32), jnp.zeros(inner_gain.shape, jnp.float32), jnp.zeros(out_weight.shape, jnp.float32))
    totals, outputs = lax.scan(one_sequence, start, (hidden_in, out_grad))
    block_out, input_grad = outputs
    norm_gain_grad, in_weight_grad, conv_weight_grad, conv_bias_grad, dt_bias_grad, a_log_grad, skip_grad, inner_gain_grad, out_weight_grad = totals
    return (block_out, input_grad, norm_gain_grad, in_weight_grad, conv_weight_grad, conv_bias_grad, dt_bias_grad, a_log_grad, skip_grad, inner_gain_grad, out_weight_grad)
```

```python
import functools

import jax
import jax.numpy as jnp
from jax import lax
from jax.experimental import pallas as pl
from jax.experimental.pallas import tpu as pltpu
from jax.sharding import PartitionSpec as P

bf16 = jnp.bfloat16
f32 = jnp.float32
highest = lax.Precision.HIGHEST
norm_eps = 1e-05
LANES = 128
CHUNK = 128
HALO = 8

VMEM = pl.BlockSpec(memory_space=pltpu.VMEM)
SMEM = pl.BlockSpec(memory_space=pltpu.SMEM)
ANY = pl.BlockSpec(memory_space=pl.ANY)


def swap(block, axis, distance):
    n = lax.axis_size(axis)
    return lax.ppermute(block, axis, [(i, i ^ distance) for i in range(n)])


def seq_gather(block):
    n = lax.axis_size("seq")
    blocks = {0: block}
    d = n // 2
    while d >= 1:
        for o in list(blocks):
            blocks[o ^ d] = swap(blocks[o], "seq", d)
        d //= 2
    return [blocks[o] for o in range(n)]


def seq_sorted(blocks):
    me = lax.axis_index("seq")
    d = 1
    while d < len(blocks):
        odd = (me // d) % 2 == 1
        blocks = [jnp.where(odd, blocks[o ^ d], blocks[o]) for o in range(len(blocks))]
        d *= 2
    return blocks


def seq_scatter(parts):
    n = lax.axis_size("seq")
    me = lax.axis_index("seq")
    d = 1
    while d < n:
        m = parts.shape[0]
        pairs = parts.reshape((m // 2, 2) + parts.shape[1:])
        bit = (me // d) % 2
        keep = lax.dynamic_index_in_dim(pairs, bit, 1, keepdims=False)
        send = lax.dynamic_index_in_dim(pairs, 1 - bit, 1, keepdims=False)
        parts = keep.astype(f32) + swap(send.astype(bf16), "seq", d).astype(f32)
        d *= 2
    return parts[0]


def all_sum(block, axis):
    n = lax.axis_size(axis)
    d = 1
    while d < n:
        block = block + swap(block, axis, d)
        d *= 2
    return block


def ring_index(place, n):
    place = lax.rem(place + 2 * n, n)
    return jnp.where(place < n // 2, 2 * place, 2 * (n - place) - 1)


def ring_place(shard, n):
    return jnp.where(shard % 2 == 0, shard // 2, n - (shard + 1) // 2)


def ring_routes(n):
    order = list(range(0, n, 2)) + list(range(n - 1, 0, -2))
    ahead = [(order[p], order[(p + 1) % n]) for p in range(n)]
    return ahead, [(b, a) for a, b in ahead]


def ring_gather(block, cut):
    n = lax.axis_size("shard")
    ahead, back = ring_routes(n)
    place = ring_place(lax.axis_index("shard"), n)
    found = [(block, lax.axis_index("shard"), 0)]
    a = b = block
    for k in range(1, n // 2):
        a = lax.ppermute(a, "shard", ahead)
        b = lax.ppermute(b, "shard", back)
        found.append((a, ring_index(place - k, n), 0))
        found.append((b, ring_index(place + k, n), 0))
    owner = ring_index(place - n // 2, n)
    found.append((lax.ppermute(a[:, :cut], "shard", ahead), owner, 0))
    found.append((lax.ppermute(b[:, cut:], "shard", back), owner, cut))
    return found


def ring_scatter(parts, cut):
    n = lax.axis_size("shard")
    ahead, back = ring_routes(n)
    place = ring_place(lax.axis_index("shard"), n)

    def pick(p, lo, hi):
        return lax.dynamic_index_in_dim(parts, ring_index(p, n), 0, keepdims=False)[:, lo:hi]

    width = parts.shape[2]
    a = pick(place - 1, 0, cut).astype(bf16)
    b = pick(place + 1, cut, width).astype(bf16)
    for k in range(1, n):
        a = lax.ppermute(a, "shard", ahead)
        b = lax.ppermute(b, "shard", back)
        a = (a.astype(f32) + pick(place - 1 - k, 0, cut)).astype(bf16)
        b = (b.astype(f32) + pick(place + 1 + k, cut, width)).astype(bf16)
    return a, b


def sigmoid(v):
    return 1.0 / (1.0 + jnp.exp(-v))


def softplus(v):
    return jnp.maximum(v, 0.0) + jnp.log1p(jnp.exp(-jnp.abs(v)))


def dot(left, right, l, r, precision=None):
    return lax.dot_general(
        left, right, (((l,), (r,)), ((), ())), preferred_element_type=f32, precision=precision
    )


def spread(per_head, hd, cols):
    rows = per_head.shape[0]
    lane = lax.broadcasted_iota(jnp.int32, (rows, LANES), 1)
    tiles = []
    per = LANES // hd
    for j in range(cols // LANES):
        tile = jnp.broadcast_to(per_head[:, j * per : j * per + 1], (rows, LANES))
        for i in range(1, per):
            h = j * per + i
            tile = jnp.where(
                lane >= i * hd, jnp.broadcast_to(per_head[:, h : h + 1], (rows, LANES)), tile
            )
        tiles.append(tile)
    return jnp.concatenate(tiles, axis=1) if len(tiles) > 1 else tiles[0]


def decay_rows(cum_t, hd, heads, state):
    last = cum_t.shape[1] - 1
    return jnp.concatenate(
        [
            jnp.broadcast_to(jnp.exp(cum_t[h : h + 1, last : last + 1]), (hd, state))
            for h in range(heads)
        ],
        axis=0,
    )


def assemble(index, copies, sems):
    handles = []
    for i, (src, dst, slot, col) in enumerate(copies):
        rows, cols = src.shape
        place = pl.multiple_of(index[slot] * rows, rows)
        handle = pltpu.make_async_copy(
            src, dst.at[pl.ds(place, rows), col : col + cols], sems.at[i]
        )
        handle.start()
        handles.append(handle)
    for handle in handles:
        handle.wait()


def decays(dt_raw, dt_bias, a_log):
    rows = dt_raw.shape[0]
    row = lax.broadcasted_iota(jnp.int32, (rows, rows), 0)
    col = lax.broadcasted_iota(jnp.int32, (rows, rows), 1)
    lower = jnp.where(row >= col, 1.0, 0.0).astype(f32)
    step = softplus(dt_raw + dt_bias)
    log_decay = -step * jnp.exp(a_log)
    cum = dot(lower, log_decay, 1, 0, highest)
    cum_t = dot(log_decay, lower, 0, 1, highest)
    return step, log_decay, cum, cum_t


def front_kernel(dims, index, *refs):
    hd, heads, cols, state, n_tok, w_cols = dims
    n_w = len(w_cols)
    tok_refs = refs[:n_tok]
    w_refs = refs[n_tok : n_tok + n_w]
    gain, conv_w, conv_b, dt_bias, a_log = refs[n_tok + n_w : n_tok + n_w + 5]
    normed, w_all, conv_in, conv_out, dt_raw, scan_out, states = refs[n_tok + n_w + 5 : -4]
    tokens, held, halo, sems = refs[-4:]
    conv_cols = cols + 2 * state
    width = 4 if conv_w.shape[0] == 4 else conv_w.shape[0]
    assemble(
        index,
        [(r, tokens, i, 0) for i, r in enumerate(tok_refs)]
        + [(r, w_all, n_tok + i, w_cols[i]) for i, r in enumerate(w_refs)],
        sems,
    )
    held[...] = jnp.zeros_like(held)
    halo[...] = jnp.zeros_like(halo)
    row = lax.broadcasted_iota(jnp.int32, (CHUNK, CHUNK), 0)
    col = lax.broadcasted_iota(jnp.int32, (CHUNK, CHUNK), 1)
    mask = row >= col
    per = LANES // hd

    @pl.loop(0, tokens.shape[0] // CHUNK)
    def _(c):
        at = pl.ds(pl.multiple_of(c * CHUNK, CHUNK), CHUNK)
        tok = tokens[at, :].astype(f32)
        rstat = lax.rsqrt(jnp.mean(tok * tok, axis=1, keepdims=True) + norm_eps)
        nrm = (tok * rstat * gain[...]).astype(bf16)
        normed[at, :] = nrm
        proj = dot(nrm, w_all[...], 1, 0)
        narrow = proj[:, :conv_cols].astype(bf16)
        conv_in[at, :] = narrow
        wide = narrow.astype(f32)
        both = jnp.concatenate([halo[...], wide], axis=0)
        halo[...] = wide[CHUNK - HALO :, :]
        first = HALO - (width - 1)
        v = conv_b[...] + conv_w[0:1, :] * both[first : first + CHUNK, :]
        for k in range(1, width):
            v = v + conv_w[k : k + 1, :] * both[first + k : first + k + CHUNK, :]
        conv_out[at, :] = v
        active = v * sigmoid(v)
        raw = proj[:, conv_cols:]
        dt_raw[at, :] = raw
        step, log_decay, cum, cum_t = decays(raw, dt_bias[...], a_log[...])
        xd = active[:, :cols] * spread(step, hd, cols)
        xd_b = xd.astype(bf16)
        b_b = active[:, cols : cols + state].astype(bf16)
        c_b = active[:, cols + state :].astype(bf16)
        cross = dot(c_b, b_b, 1, 1)
        before = held[...]
        before_b = before.astype(bf16)
        states[c] = before_b
        tiles = []
        for j in range(cols // LANES):
            tile = None
            for i in range(per):
                h = j * per + i
                gap = cum[:, h : h + 1] - cum_t[h : h + 1, :]
                kern = (jnp.exp(jnp.where(mask, gap, -1e30)) * cross).astype(bf16)
                out = dot(kern, xd_b[:, j * LANES : (j + 1) * LANES], 1, 0)
                tile = out if tile is None else jnp.where(col >= i * hd, out, tile)
            tiles.append(tile)
        intra = jnp.concatenate(tiles, axis=1) if len(tiles) > 1 else tiles[0]
        inter = spread(jnp.exp(cum), hd, cols) * dot(c_b, before_b, 1, 1)
        scan_out[at, :] = intra + inter
        tail = jnp.exp(cum[CHUNK - 1 : CHUNK, :] - cum)
        xt = (xd * spread(tail, hd, cols)).astype(bf16)
        held[...] = decay_rows(cum_t, hd, heads, state) * before + dot(xt, b_b, 0, 0)


def gate_kernel(dims, index, *refs):
    cols, n_tok, w_cols, z_width = dims
    n_w = len(w_cols)
    cot_refs = refs[:n_tok]
    w_refs = refs[n_tok : n_tok + n_w]
    normed, conv_out, scan_out, skip, gain = refs[n_tok + n_w : n_tok + n_w + 5]
    cotan, wz, wo, gate, gated_in, d_gated, sums = refs[n_tok + n_w + 5 : -1]
    sems = refs[-1]
    copies = [(r, cotan, i, 0) for i, r in enumerate(cot_refs)]
    assemble_two(index, copies, w_refs, w_cols, n_tok, wz, wo, sems)
    lane = lax.broadcasted_iota(jnp.int32, (CHUNK, CHUNK), 1)

    @pl.loop(0, normed.shape[0] // CHUNK)
    def _(c):
        at = pl.ds(pl.multiple_of(c * CHUNK, CHUNK), CHUNK)
        z = dot(normed[at, :], wz[...], 1, 0)
        dg = dot(cotan[at, :], wo[...], 1, 1)
        v = conv_out[at, :cols]
        mixed = scan_out[at, :] + skip[...] * (v * sigmoid(v))
        gi = mixed * (z * sigmoid(z))
        gate[at, :] = z
        gated_in[at, :] = gi
        d_gated[at, :] = dg
        squares = jnp.sum(gi * gi, axis=1, keepdims=True)
        slopes = jnp.sum(gi * dg * gain[...], axis=1, keepdims=True)
        both = jnp.where(lane == 0, squares, jnp.where(lane == 1, slopes, 0.0))
        sums[:, at] = jnp.transpose(both)[:8, :]


def assemble_two(index, copies, w_refs, w_cols, first, wz, wo, sems):
    rows = w_refs[0].shape[0]
    z_width = wz.shape[1]
    handles = []

    def start(src, dst):
        handle = pltpu.make_async_copy(src, dst, sems.at[len(handles)])
        handle.start()
        handles.append(handle)

    for src, dst, slot, col in copies:
        size = src.shape[0]
        start(src, dst.at[pl.ds(pl.multiple_of(index[slot] * size, size), size), :])
    half = z_width // 2
    steps = wo.shape[1] // half
    per = wo.shape[0] // (2 * rows)
    for i, src in enumerate(w_refs):
        owner = index[first + i]
        col = w_cols[i]
        if col == 0:
            part = src if src.shape[1] == z_width else src.at[:, 0:z_width]
            start(part, wz.at[pl.ds(pl.multiple_of(owner * rows, rows), rows), :])
        if col + src.shape[1] == 2 * z_width:
            at = 0 if col else z_width
            band = pl.multiple_of(lax.rem(owner, per) * (2 * rows), 2 * rows)
            column = pl.multiple_of(lax.div(owner, per) * half, half)
            for t in range(2):
                start(
                    src.at[:, at + t * half : at + (t + 1) * half],
                    wo.at[pl.ds(band + t * rows, rows), pl.ds(column, half)],
                )
    for handle in handles:
        handle.wait()


def turn_kernel(dims, gate, gated_in, d_gated, conv_out, scan_out, sums, skip, gain, *outs):
    cols, inner = dims
    gated, d_gate, d_mixed, gain_grad = outs
    gain_grad[...] = jnp.zeros_like(gain_grad)

    @pl.loop(0, gate.shape[0] // CHUNK)
    def _(c):
        at = pl.ds(pl.multiple_of(c * CHUNK, CHUNK), CHUNK)
        stat = jnp.transpose(sums[:, at])
        scale = lax.rsqrt(stat[:, 0:1] / inner + norm_eps)
        slope = scale * scale * scale * (stat[:, 1:2] / inner)
        gi = gated_in[at, :]
        dg = d_gated[at, :]
        scaled = gi * scale
        gated[at, :] = (scaled * gain[...]).astype(bf16)
        gain_grad[...] += jnp.sum(dg * scaled, axis=0, keepdims=True)
        d_gi = scale * (gain[...] * dg) - gi * slope
        z = gate[at, :]
        sig = sigmoid(z)
        v = conv_out[at, :cols]
        mixed = scan_out[at, :] + skip[...] * (v * sigmoid(v))
        d_mixed[at, :] = d_gi * (z * sig)
        d_gate[at, :] = (d_gi * mixed * (sig * (1.0 + z * (1.0 - sig)))).astype(bf16)


def back_kernel(dims, *refs):
    hd, heads, cols, state = dims
    conv_in, conv_out, dt_raw, scan_out, states, d_mixed = refs[:6]
    conv_w, dt_bias, a_log, skip, picks = refs[6:11]
    d_proj, conv_grad, head_grad = refs[11:14]
    held, halo = refs[14:]
    conv_cols = cols + 2 * state
    width = conv_w.shape[0]
    held[...] = jnp.zeros_like(held)
    halo[...] = jnp.zeros_like(halo)
    conv_grad[...] = jnp.zeros_like(conv_grad)
    head_grad[...] = jnp.zeros_like(head_grad)
    row = lax.broadcasted_iota(jnp.int32, (CHUNK, CHUNK), 0)
    col = lax.broadcasted_iota(jnp.int32, (CHUNK, CHUNK), 1)
    mask = row >= col
    upper = jnp.where(row <= col, 1.0, 0.0).astype(f32)
    per = LANES // hd
    chunks = conv_in.shape[0] // CHUNK

    @pl.loop(0, chunks)
    def _(turn):
        c = chunks - 1 - turn
        at = pl.ds(pl.multiple_of(c * CHUNK, CHUNK), CHUNK)
        v = conv_out[at, :]
        sig = sigmoid(v)
        active = v * sig
        raw = dt_raw[at, :]
        step, log_decay, cum, cum_t = decays(raw, dt_bias[...], a_log[...])
        step_s = spread(step, hd, cols)
        x = active[:, :cols]
        xd = x * step_s
        xd_b = xd.astype(bf16)
        b_b = active[:, cols : cols + state].astype(bf16)
        c_b = active[:, cols + state :].astype(bf16)
        cross = dot(c_b, b_b, 1, 1)
        dm = d_mixed[at, :]
        dy_b = dm.astype(bf16)
        before_b = states[c]
        later = held[...]
        later_b = later.astype(bf16)
        d_cross = jnp.zeros((CHUNK, CHUNK), f32)
        tiles = []
        for j in range(cols // LANES):
            tile = None
            dm_tile = dm[:, j * LANES : (j + 1) * LANES]
            for i in range(per):
                h = j * per + i
                gap = cum[:, h : h + 1] - cum_t[h : h + 1, :]
                fall = jnp.exp(jnp.where(mask, gap, -1e30))
                kern = (fall * cross).astype(bf16)
                out = dot(kern, dy_b[:, j * LANES : (j + 1) * LANES], 0, 0)
                tile = out if tile is None else jnp.where(col >= i * hd, out, tile)
                own = (col >= i * hd) & (col < (i + 1) * hd)
                dy_h = jnp.where(own, dm_tile, 0.0).astype(bf16)
                d_cross = d_cross + fall * dot(dy_h, xd_b[:, j * LANES : (j + 1) * LANES], 1, 1)
            tiles.append(tile)
        intra = jnp.concatenate(tiles, axis=1) if len(tiles) > 1 else tiles[0]
        d_cross_b = d_cross.astype(bf16)
        grown = spread(jnp.exp(cum), hd, cols)
        dy_g = (dm * grown).astype(bf16)
        tail_s = spread(jnp.exp(cum[CHUNK - 1 : CHUNK, :] - cum), hd, cols)
        xt = (xd * tail_s).astype(bf16)
        d_c = dot(d_cross_b, b_b, 1, 0) + dot(dy_g, before_b, 1, 0)
        d_b = dot(d_cross_b, c_b, 0, 0) + dot(xt, later_b, 1, 0)
        inter = tail_s * dot(b_b, later_b, 1, 1)
        held[...] = decay_rows(cum_t, hd, heads, state) * later + dot(dy_g, c_b, 0, 0)
        d_xd = intra + inter
        carried = xd * inter
        change = (
            dy_b.astype(f32) * scan_out[at, :] - xd_b.astype(f32) * intra - carried
        )
        change_h = dot(change, picks[...], 1, 0, highest)
        step_h = dot(x * d_xd, picks[...], 1, 0, highest)
        skip_h = dot(jnp.sum(dm * x, axis=0, keepdims=True), picks[...], 1, 0, highest)
        ones = jnp.ones((8, state), f32)
        kept = dot(ones, before_b.astype(f32) * later, 1, 1, highest)
        kept_h = dot(kept, picks[...], 1, 0, highest)[0:1, :]
        carried_h = dot(jnp.sum(carried, axis=0, keepdims=True), picks[...], 1, 0, highest)
        d_log = (
            dot(upper, change_h, 1, 0, highest)
            + jnp.exp(cum[CHUNK - 1 : CHUNK, :]) * kept_h
            + carried_h
        )
        d_step = step_h - d_log * jnp.exp(a_log[...])
        d_raw = jnp.where(col < heads, d_step * sigmoid(raw + dt_bias[...]), 0.0)
        head_grad[0:1, :] += jnp.sum(d_raw, axis=0, keepdims=True)
        head_grad[1:2, :] += jnp.sum(d_log * log_decay, axis=0, keepdims=True)
        head_grad[2:3, :] += skip_h
        d_x = step_s * d_xd + skip[...] * dm
        d_active = jnp.concatenate([d_x, d_b, d_c], axis=1)
        d_v = d_active * (sig * (1.0 + v * (1.0 - sig)))
        both = jnp.concatenate([d_v, halo[...]], axis=0)
        halo[...] = d_v[:HALO, :]
        entered = conv_in[at, :].astype(f32)
        d_in = None
        for k in range(width):
            shifted = both[width - 1 - k : width - 1 - k + CHUNK, :]
            term = conv_w[k : k + 1, :] * shifted
            d_in = term if d_in is None else d_in + term
            conv_grad[k : k + 1, :] += jnp.sum(entered * shifted, axis=0, keepdims=True)
        conv_grad[width : width + 1, :] += jnp.sum(d_v, axis=0, keepdims=True)
        d_proj[at, :conv_cols] = d_in.astype(bf16)
        d_proj[at, conv_cols:] = d_raw.astype(bf16)


def shaped(shape, kind):
    return jax.ShapeDtypeStruct(shape, kind)


def body(
    hidden_in,
    norm_gain,
    in_weight,
    conv_weight,
    conv_bias,
    dt_bias,
    a_log,
    skip,
    inner_gain,
    out_weight,
    out_grad,
):
    n_seq = lax.axis_size("seq")
    n_shard = lax.axis_size("shard")
    me = lax.axis_index("seq")
    own = hidden_in[0]
    cotan_own = out_grad[0]
    rows, model = own.shape
    length = rows * n_seq
    inner = inner_gain.shape[0]
    conv_dim = conv_bias.shape[0]
    width = conv_weight.shape[0]
    heads_all = dt_bias.shape[0]
    hd = inner // heads_all
    state = (conv_dim - inner) // 2
    cols = inner // n_seq
    heads = heads_all // n_seq
    deep = in_weight.shape[0]
    conv_cols = cols + 2 * state
    one = conv_cols + LANES
    chunks = length // CHUNK

    def columns(array, start, size):
        return lax.dynamic_slice_in_dim(array, start, size, axis=array.ndim - 1)

    w_dt = columns(in_weight, inner + conv_dim + me * heads, heads)
    slab_one = jnp.concatenate(
        [
            columns(in_weight, inner + me * cols, cols),
            in_weight[:, 2 * inner : 2 * inner + 2 * state],
            jnp.pad(w_dt, ((0, 0), (0, LANES - heads))),
        ],
        axis=1,
    )
    bands = n_shard // n_seq
    strip = model // n_seq
    route = [
        (q * n_shard + s, (s // bands) * n_shard + q * bands + s % bands)
        for s in range(n_shard)
        for q in range(n_seq)
    ]
    out_rows = out_weight.shape[0]
    strips = out_weight.reshape(out_rows, n_seq, strip)
    sent = lax.dynamic_index_in_dim(strips, me, 1, keepdims=False)
    tile = lax.ppermute(sent, ("seq", "shard"), route)
    slab_two = jnp.concatenate(
        [columns(in_weight, me * cols, cols), tile[:deep], tile[deep:]], axis=1
    )

    tok_blocks = seq_gather(own)
    cut_one = one // LANES // 2 * LANES
    ring_one = ring_gather(slab_one, cut_one)
    cot_blocks = seq_gather(cotan_own.astype(bf16))
    ring_two = ring_gather(slab_two, cols)

    places = [me ^ o for o in range(n_seq)]
    conv_w = jnp.concatenate([columns(conv_weight, me * cols, cols), conv_weight[:, inner:]], 1)
    conv_b = jnp.concatenate([columns(conv_bias, me * cols, cols), conv_bias[inner:]])[None]
    pad_heads = lambda a: jnp.pad(columns(a, me * heads, heads), (0, LANES - heads))[None]
    dt_bias_h = pad_heads(dt_bias)
    a_log_h = pad_heads(a_log)
    skip_s = jnp.repeat(columns(skip, me * heads, heads), hd)[None]
    gain_s = columns(inner_gain, me * cols, cols)[None]
    picks = jnp.where(jnp.arange(cols)[:, None] // hd == jnp.arange(LANES)[None, :], 1.0, 0.0)
    picks = picks.astype(f32)

    index_one = jnp.stack(places + [o for _, o, _ in ring_one]).astype(jnp.int32)
    n_one = len(ring_one)
    normed, w_one, conv_in, conv_out, dt_raw, scan_out, states = pl.pallas_call(
        functools.partial(
            front_kernel, (hd, heads, cols, state, n_seq, tuple(c for _, _, c in ring_one))
        ),
        name="front",
        in_specs=[SMEM] + [ANY] * (n_seq + n_one) + [VMEM] * 5,
        out_specs=[VMEM] * 7,
        out_shape=[
            shaped((length, model), bf16),
            shaped((model, one), bf16),
            shaped((length, conv_cols), bf16),
            shaped((length, conv_cols), f32),
            shaped((length, LANES), f32),
            shaped((length, cols), f32),
            shaped((chunks, cols, state), bf16),
        ],
        scratch_shapes=[
            pltpu.VMEM((length, model), bf16),
            pltpu.VMEM((cols, state), f32),
            pltpu.VMEM((HALO, conv_cols), f32),
            pltpu.SemaphoreType.DMA((n_seq + n_one,)),
        ],
        cost_estimate=pl.CostEstimate(
            flops=2 * length * model * one + 8 * length * CHUNK * cols,
            bytes_accessed=12 * length * model,
            transcendentals=length * CHUNK * heads,
        ),
    )(
        index_one,
        *tok_blocks,
        *[b for b, _, _ in ring_one],
        norm_gain[None],
        conv_w,
        conv_b,
        dt_bias_h,
        a_log_h,
    )

    index_two = jnp.stack(places + [o for _, o, _ in ring_two]).astype(jnp.int32)
    n_two = len(ring_two)
    cotan, w_z, w_o, gate, gated_in, d_gated, sums = pl.pallas_call(
        functools.partial(
            gate_kernel, (cols, n_seq, tuple(c for _, _, c in ring_two), cols)
        ),
        name="gate",
        in_specs=[SMEM] + [ANY] * (n_seq + n_two) + [VMEM] * 5,
        out_specs=[VMEM] * 7,
        out_shape=[
            shaped((length, model), bf16),
            shaped((model, cols), bf16),
            shaped((cols, model), bf16),
            shaped((length, cols), f32),
            shaped((length, cols), f32),
            shaped((length, cols), f32),
            shaped((8, length), f32),
        ],
        scratch_shapes=[pltpu.SemaphoreType.DMA((n_seq + 3 * n_two,))],
        cost_estimate=pl.CostEstimate(
            flops=4 * length * model * cols,
            bytes_accessed=14 * length * model,
            transcendentals=2 * length * cols,
        ),
    )(
        index_two,
        *cot_blocks,
        *[b for b, _, _ in ring_two],
        normed,
        conv_out,
        scan_out,
        skip_s,
        gain_s,
    )

    sums = all_sum(sums, "seq")
    gated, d_gate, d_mixed, gain_part = pl.pallas_call(
        functools.partial(turn_kernel, (cols, inner)),
        name="turn",
        in_specs=[VMEM] * 8,
        out_specs=[VMEM] * 4,
        out_shape=[
            shaped((length, cols), bf16),
            shaped((length, cols), bf16),
            shaped((length, cols), f32),
            shaped((1, cols), f32),
        ],
        cost_estimate=pl.CostEstimate(
            flops=30 * length * cols, bytes_accessed=30 * length * cols, transcendentals=0
        ),
    )(gate, gated_in, d_gated, conv_out, scan_out, sums, skip_s, gain_s)

    out_parts = jnp.dot(gated, w_o, preferred_element_type=f32)
    block_out = own.astype(f32) + seq_scatter(out_parts.reshape(n_seq, rows, model))

    z_grad = dot(normed, d_gate, 0, 0).reshape(n_shard, deep, cols)
    o_grad = dot(gated, cotan, 0, 0)
    o_grad = o_grad.reshape(bands, 2, deep, n_seq, strip).transpose(3, 0, 2, 1, 4)
    o_grad = o_grad.reshape(n_shard, deep, cols)
    z_own, o_own = ring_scatter(jnp.concatenate([z_grad, o_grad], axis=2), cols)
    o_own = jnp.concatenate([o_own[:, :strip], o_own[:, strip:]], axis=0)
    o_own = lax.ppermute(o_own, ("seq", "shard"), [(b, a) for a, b in route])
    o_all = seq_sorted(seq_gather(o_own))
    z_all = seq_sorted(seq_gather(z_own))
    out_weight_grad = jnp.concatenate(o_all, axis=1).astype(f32)

    d_proj, conv_part, head_part = pl.pallas_call(
        functools.partial(back_kernel, (hd, heads, cols, state)),
        name="back",
        in_specs=[VMEM] * 11,
        out_specs=[VMEM] * 3,
        out_shape=[
            shaped((length, one), bf16),
            shaped((8, conv_cols), f32),
            shaped((8, LANES), f32),
        ],
        scratch_shapes=[pltpu.VMEM((cols, state), f32), pltpu.VMEM((HALO, conv_cols), f32)],
        cost_estimate=pl.CostEstimate(
            flops=20 * length * CHUNK * cols,
            bytes_accessed=14 * length * model,
            transcendentals=length * CHUNK * heads,
        ),
    )(
        conv_in,
        conv_out,
        dt_raw,
        scan_out,
        states,
        d_mixed,
        conv_w,
        dt_bias_h,
        a_log_h,
        skip_s,
        picks,
    )

    one_parts = dot(normed, d_proj, 0, 0).reshape(n_shard, deep, one)
    one_a, one_b = ring_scatter(one_parts, cut_one)
    one_all = seq_sorted(seq_gather(jnp.concatenate([one_a, one_b], axis=1)))

    d_normed = dot(d_proj, w_one, 1, 1) + dot(d_gate, w_z, 1, 1)
    norm_part = jnp.sum(d_normed * normed.astype(f32), axis=0) / norm_gain
    d_own = seq_scatter(d_normed.reshape(n_seq, rows, model))
    own_f = own.astype(f32)
    rstat = lax.rsqrt(jnp.mean(own_f * own_f, axis=-1, keepdims=True) + norm_eps)
    scaled = norm_gain * d_own
    input_grad = (
        cotan_own
        + rstat * scaled
        - own_f * rstat * rstat * rstat * jnp.mean(scaled * own_f, axis=-1, keepdims=True)
    )

    packed = jnp.concatenate(
        [
            conv_part.reshape(-1),
            head_part.reshape(-1),
            gain_part.reshape(-1),
            norm_part,
        ]
    ).reshape(-1, LANES)
    packs = [p.reshape(-1) for p in seq_sorted(seq_gather(all_sum(packed, "shard")))]
    edges = [8 * conv_cols, 8 * LANES, cols, model]
    convs, head_parts, gains, norms = [], [], [], []
    for p in packs:
        at = 0
        for size, bin_ in zip(edges, (convs, head_parts, gains, norms)):
            bin_.append(p[at : at + size])
            at += size
    convs = [c.reshape(8, conv_cols) for c in convs]
    head_parts = [h.reshape(8, LANES) for h in head_parts]
    conv_all = jnp.concatenate([c[:, :cols] for c in convs] + [sum(c[:, cols:] for c in convs)], 1)
    head_all = jnp.concatenate([h[:, :heads] for h in head_parts], axis=1)

    shared = sum(o[:, cols:conv_cols].astype(f32) for o in one_all)
    in_weight_grad = jnp.concatenate(
        [z.astype(f32) for z in z_all]
        + [o[:, :cols].astype(f32) for o in one_all]
        + [shared]
        + [o[:, conv_cols : conv_cols + heads].astype(f32) for o in one_all],
        axis=1,
    )
    return (
        block_out[None],
        input_grad[None],
        sum(norms),
        in_weight_grad,
        conv_all[:width],
        conv_all[width],
        head_all[0],
        head_all[1],
        head_all[2],
        jnp.concatenate(gains),
        out_weight_grad,
    )


def solution(mesh):
    tokens = P("shard", "seq", None)
    rows = P("shard", None)
    return jax.shard_map(
        body,
        mesh=mesh,
        in_specs=(tokens, P(), rows, P(), P(), P(), P(), P(), P(), rows, tokens),
        out_specs=(tokens, tokens, P(), rows, P(), P(), P(), P(), P(), P(), rows),
        check_vma=False,
    )
```

```python
import functools

import jax
import jax.numpy as jnp
from jax import lax
from jax.experimental import pallas as pl
from jax.experimental.pallas import tpu as pltpu
from jax.sharding import PartitionSpec as P


bf16 = jnp.bfloat16
f32 = jnp.float32
norm_eps = 1e-05
LANES = 128
CHUNK = 128
HALO = 8
FRONT_PIECES = 4
BACK_PIECES = 2

VMEM = pl.BlockSpec(memory_space=pltpu.VMEM)
SMEM = pl.BlockSpec(memory_space=pltpu.SMEM)
ANY = pl.BlockSpec(memory_space=pl.ANY)


def swap(block, axis, distance):
    n = lax.axis_size(axis)
    return lax.ppermute(block, axis, [(i, i ^ distance) for i in range(n)])


def seq_gather(block):
    n = lax.axis_size("seq")
    blocks = {0: block}
    d = n // 2
    while d >= 1:
        for o in list(blocks):
            blocks[o ^ d] = swap(blocks[o], "seq", d)
        d //= 2
    return [blocks[o] for o in range(n)]


def seq_scatter(parts):
    n = lax.axis_size("seq")
    me = lax.axis_index("seq")
    d = 1
    while d < n:
        m = parts.shape[0]
        pairs = parts.reshape((m // 2, 2) + parts.shape[1:])
        bit = (me // d) % 2
        keep = lax.dynamic_index_in_dim(pairs, bit, 1, keepdims=False)
        send = lax.dynamic_index_in_dim(pairs, 1 - bit, 1, keepdims=False)
        got = swap(send.astype(bf16), "seq", d)
        parts = keep.astype(f32) + got.astype(f32)
        d *= 2
    return parts[0]


def all_sum(block, axis):
    n = lax.axis_size(axis)
    d = 1
    while d < n:
        got = swap(block, axis, d)
        block = block + got
        d *= 2
    return block


def ring_index(place, n):
    place = lax.rem(place + 2 * n, n)
    return jnp.where(place < n // 2, 2 * place, 2 * (n - place) - 1)


def ring_place(shard, n):
    return jnp.where(shard % 2 == 0, shard // 2, n - (shard + 1) // 2)


def ring_routes(n):
    order = list(range(0, n, 2)) + list(range(n - 1, 0, -2))
    ahead = [(order[p], order[(p + 1) % n]) for p in range(n)]
    return ahead, [(b, a) for a, b in ahead]


class RingGather:
    def __init__(self, block, cut):
        n = lax.axis_size("shard")
        self.n, self.cut, self.hop = n, cut, 0
        self.ahead, self.back = ring_routes(n)
        self.place = ring_place(lax.axis_index("shard"), n)
        self.a = self.b = block
        self.found = [(block, lax.axis_index("shard"), 0)]

    def step(self):
        if self.hop == self.n // 2:
            return []
        self.hop += 1
        k, n = self.hop, self.n
        if k == n // 2:
            self.a = lax.ppermute(self.a[:, : self.cut], "shard", self.ahead)
            self.b = lax.ppermute(self.b[:, self.cut :], "shard", self.back)
            owner = ring_index(self.place - k, n)
            self.found += [(self.a, owner, 0), (self.b, owner, self.cut)]
        else:
            self.a = lax.ppermute(self.a, "shard", self.ahead)
            self.b = lax.ppermute(self.b, "shard", self.back)
            self.found.append((self.a, ring_index(self.place - k, n), 0))
            self.found.append((self.b, ring_index(self.place + k, n), 0))
        return [self.a, self.b]


def bit_orders(n):
    bits = list(range(n.bit_length() - 1))
    return bits, [bits[1], bits[0]] + bits[2:]


def slot(owner, bits):
    place = 0
    for b in bits:
        place = 2 * place + ((owner >> b) & 1)
    return place


class Halving:
    def __init__(self, slabs):
        self.slabs = list(slabs)
        self.orders = bit_orders(lax.axis_size("shard"))
        self.hop = 0

    def step(self):
        if self.hop == len(self.orders[0]):
            return []
        me = lax.axis_index("shard")
        for i, slab in enumerate(self.slabs):
            b = self.orders[i][self.hop]
            pair = slab.reshape((2, slab.shape[0] // 2) + slab.shape[1:])
            bit = (me >> b) & 1
            keep = lax.dynamic_index_in_dim(pair, bit, 0, keepdims=False)
            send = lax.dynamic_index_in_dim(pair, 1 - bit, 0, keepdims=False)
            got = swap(send, "shard", 1 << b)
            self.slabs[i] = (keep.astype(f32) + got.astype(f32)).astype(bf16)
        self.hop += 1
        return self.slabs

    def finish(self):
        while self.step():
            pass
        return [s[0] for s in self.slabs]


def sigmoid(v):
    return 1.0 / (1.0 + jnp.exp(-v))


def softplus(v):
    return jnp.maximum(v, 0.0) + jnp.log1p(jnp.exp(-jnp.abs(v)))


def dot(left, right, l, r, precision=None):
    return lax.dot_general(
        left, right, (((l,), (r,)), ((), ())), preferred_element_type=f32, precision=precision
    )


def exact(left, right, l, r):
    total = None
    whole, ones = (right, left) if left.dtype == bf16 else (left, right)
    for _ in range(3):
        piece = whole.astype(bf16)
        whole = whole - piece.astype(f32)
        pair = (ones, piece) if left.dtype == bf16 else (piece, ones)
        term = dot(*pair, l, r)
        total = term if total is None else total + term
    return total


def spread(per_head, hd, cols):
    rows = per_head.shape[0]
    lane = lax.broadcasted_iota(jnp.int32, (rows, LANES), 1)
    tiles = []
    per = LANES // hd
    for j in range(cols // LANES):
        tile = jnp.broadcast_to(per_head[:, j * per : j * per + 1], (rows, LANES))
        for i in range(1, per):
            h = j * per + i
            tile = jnp.where(
                lane >= i * hd, jnp.broadcast_to(per_head[:, h : h + 1], (rows, LANES)), tile
            )
        tiles.append(tile)
    return jnp.concatenate(tiles, axis=1) if len(tiles) > 1 else tiles[0]


def decay_rows(cum_t, hd, heads, state):
    last = cum_t.shape[1] - 1
    return jnp.concatenate(
        [
            jnp.broadcast_to(jnp.exp(cum_t[h : h + 1, last : last + 1]), (hd, state))
            for h in range(heads)
        ],
        axis=0,
    )


def assemble(copies, sems):
    handles = []
    for i, (src, dst, owner, col) in enumerate(copies):
        rows, cols = src.shape
        place = pl.multiple_of(owner * rows, rows)
        handle = pltpu.make_async_copy(
            src, dst.at[pl.ds(place, rows), col : col + cols], sems.at[i]
        )
        handle.start()
        handles.append(handle)
    for handle in handles:
        handle.wait()


def ring_owners(shard, n, cut):
    place = ring_place(shard, n)
    found = [(shard, 0)]
    for k in range(1, n // 2):
        found.append((ring_index(place - k, n), 0))
        found.append((ring_index(place + k, n), 0))
    last = ring_index(place - n // 2, n)
    return found + [(last, 0), (last, cut)]


def own_heads(table, me, heads):
    return pltpu.roll(table[...], lax.rem(LANES - me * heads, LANES), 1)


def own_columns(ref, me, cols, inner):
    mine = ref[:, pl.ds(pl.multiple_of(me * cols, LANES), cols)]
    if inner == ref.shape[1]:
        return mine
    return jnp.concatenate([mine, ref[:, inner:]], axis=1)


def decays(dt_raw, dt_bias, a_log):
    rows = dt_raw.shape[0]
    row = lax.broadcasted_iota(jnp.int32, (rows, rows), 0)
    col = lax.broadcasted_iota(jnp.int32, (rows, rows), 1)
    lower = jnp.where(row >= col, 1.0, 0.0).astype(bf16)
    step = softplus(dt_raw + dt_bias)
    log_decay = -step * jnp.exp(a_log)
    cum = exact(lower, log_decay, 1, 0)
    cum_t = jnp.transpose(cum)
    return step, log_decay, cum, cum_t


def front_kernel(dims, ids, *refs):
    hd, heads, cols, state, inner, n_seq, n_shard, w_cut, n_skip = dims
    conv_cols = cols + 2 * state
    me = ids[0]
    step = pl.program_id(0)
    if n_skip is None:
        n_w = n_shard + 1
        tok_refs = refs[:n_seq]
        w_refs = refs[n_seq : n_seq + n_w]
        gain, conv_w_all, conv_b_all, table = refs[n_seq + n_w : n_seq + n_w + 4]
        tokens_all, w_all = refs[n_seq + n_w + 4 : n_seq + n_w + 6]
        normed, conv_in, conv_out, dt_raw, scan_out, states, held, halo = refs[-10:-2]
        sems, projected = refs[-2:]

        @pl.when(step == 0)
        def _():
            owners = ring_owners(ids[1], n_shard, w_cut)
            assemble(
                [(r, tokens_all, me ^ o, 0) for o, r in enumerate(tok_refs)]
                + [(r, w_all, o, c) for r, (o, c) in zip(w_refs, owners)],
                sems,
            )
            held[...] = jnp.zeros_like(held)
            halo[...] = jnp.zeros_like(halo)

        size = normed.shape[0]
        tok = tokens_all[pl.ds(pl.multiple_of(step * size, size), size), :].astype(f32)
    else:
        tokens, w_all, gain, conv_w_all, conv_b_all, table, held_in, halo_in = refs[:8]
        normed, conv_in, conv_out, dt_raw, scan_out, states, held, halo, projected = refs[
            8 + n_skip :
        ]

        @pl.when(step == 0)
        def _():
            held[...] = held_in[...]
            halo[...] = halo_in[...]

        tok = tokens[...].astype(f32)
    conv_w = own_columns(conv_w_all, me, cols, inner)
    conv_b = own_columns(conv_b_all, me, cols, inner)
    by_head = own_heads(table, me, heads)
    dt_bias, a_log = by_head[0:1, :], by_head[1:2, :]
    width = conv_w.shape[0]
    row = lax.broadcasted_iota(jnp.int32, (CHUNK, CHUNK), 0)
    col = lax.broadcasted_iota(jnp.int32, (CHUNK, CHUNK), 1)
    mask = row >= col
    per = LANES // hd

    rstat = lax.rsqrt(jnp.mean(tok * tok, axis=1, keepdims=True) + norm_eps)
    nrm = (tok * rstat * gain[...]).astype(bf16)
    normed[...] = nrm
    projected[...] = dot(nrm, w_all[...], 1, 0)

    @pl.loop(0, normed.shape[0] // CHUNK)
    def _(c):
        at = pl.ds(pl.multiple_of(c * CHUNK, CHUNK), CHUNK)
        proj = projected[at, :]
        narrow = proj[:, :conv_cols].astype(bf16)
        conv_in[at, :] = narrow
        wide = narrow.astype(f32)
        both = jnp.concatenate([halo[...], wide], axis=0)
        halo[...] = wide[CHUNK - HALO :, :]
        first = HALO - (width - 1)
        v = conv_b + conv_w[0:1, :] * both[first : first + CHUNK, :]
        for k in range(1, width):
            v = v + conv_w[k : k + 1, :] * both[first + k : first + k + CHUNK, :]
        conv_out[at, :] = v
        active = v * sigmoid(v)
        raw = proj[:, conv_cols:]
        dt_raw[at, :] = raw
        step, _, cum, cum_t = decays(raw, dt_bias, a_log)
        xd = active[:, :cols] * spread(step, hd, cols)
        xd_b = xd.astype(bf16)
        b_b = active[:, cols : cols + state].astype(bf16)
        c_b = active[:, cols + state :].astype(bf16)
        cross = dot(c_b, b_b, 1, 1)
        before = held[...]
        before_b = before.astype(bf16)
        states[c] = before_b
        tiles = []
        for j in range(cols // LANES):
            tile = None
            for i in range(per):
                h = j * per + i
                gap = cum[:, h : h + 1] - cum_t[h : h + 1, :]
                kern = (jnp.exp(jnp.where(mask, gap, -1e30)) * cross).astype(bf16)
                out = dot(kern, xd_b[:, j * LANES : (j + 1) * LANES], 1, 0)
                tile = out if tile is None else jnp.where(col >= i * hd, out, tile)
            tiles.append(tile)
        intra = jnp.concatenate(tiles, axis=1) if len(tiles) > 1 else tiles[0]
        inter = spread(jnp.exp(cum), hd, cols) * dot(c_b, before_b, 1, 1)
        scan_out[at, :] = intra + inter
        tail = jnp.exp(cum[CHUNK - 1 : CHUNK, :] - cum)
        xt = (xd * spread(tail, hd, cols)).astype(bf16)
        held[...] = decay_rows(cum_t, hd, heads, state) * before + dot(xt, b_b, 0, 0)


def gate_kernel(dims, ids, *refs):
    cols, heads, hd, n_seq, n_shard = dims
    n_w = n_shard + 1
    me = ids[0]
    cot_refs = refs[:n_seq]
    w_refs = refs[n_seq : n_seq + n_w]
    normed, conv_out, scan_out, table, gain_all = refs[n_seq + n_w : n_seq + n_w + 5]
    cotan, wz, wo, gate, mixed_out, d_gated, sums, sems = refs[n_seq + n_w + 5 :]
    step = pl.program_id(0)

    @pl.when(step == 0)
    def _():
        copies = [(r, cotan, me ^ o) for o, r in enumerate(cot_refs)]
        assemble_two(copies, w_refs, ring_owners(ids[1], n_shard, cols), wz, wo, sems)

    skip = spread(own_heads(table, me, heads), hd, cols)[2:3, :]
    gain = own_columns(gain_all, me, cols, gain_all.shape[1])
    size = normed.shape[0]
    lane = lax.broadcasted_iota(jnp.int32, (size, LANES), 1)
    z = dot(normed[...], wz[...], 1, 0)
    dg = dot(cotan[pl.ds(pl.multiple_of(step * size, size), size), :], wo[...], 1, 1)
    v = conv_out[...]
    mixed = scan_out[...] + skip * (v * sigmoid(v))
    gi = mixed * (z * sigmoid(z))
    gate[...] = z
    mixed_out[...] = mixed
    d_gated[...] = dg
    squares = jnp.sum(gi * gi, axis=1, keepdims=True)
    slopes = jnp.sum(gi * dg * gain, axis=1, keepdims=True)
    both = jnp.where(lane == 0, squares, jnp.where(lane == 1, slopes, 0.0))
    sums[...] = jnp.transpose(both)[:8, :]


def assemble_two(copies, w_refs, owners, wz, wo, sems):
    rows = w_refs[0].shape[0]
    z_width = wz.shape[1]
    handles = []

    def start(src, dst):
        handle = pltpu.make_async_copy(src, dst, sems.at[len(handles)])
        handle.start()
        handles.append(handle)

    for src, dst, place in copies:
        size = src.shape[0]
        start(src, dst.at[pl.ds(pl.multiple_of(place * size, size), size), :])
    half = z_width // 2
    per = wo.shape[0] // (2 * rows)
    for src, (owner, col) in zip(w_refs, owners):
        if col == 0:
            part = src if src.shape[1] == z_width else src.at[:, 0:z_width]
            start(part, wz.at[pl.ds(pl.multiple_of(owner * rows, rows), rows), :])
        if col + src.shape[1] == 2 * z_width:
            at = 0 if col else z_width
            band = pl.multiple_of(lax.rem(owner, per) * (2 * rows), 2 * rows)
            column = pl.multiple_of(lax.div(owner, per) * half, half)
            for t in range(2):
                start(
                    src.at[:, at + t * half : at + (t + 1) * half],
                    wo.at[pl.ds(band + t * rows, rows), pl.ds(column, half)],
                )
    for handle in handles:
        handle.wait()


def turn_kernel(dims, ids, *refs):
    cols, inner, _, _ = dims
    gate, mixed_in, d_gated, sums, gain_all, normed, cotan, w_o = refs[:8]
    gated, d_gate, d_mixed, gain_grad, out_part, z_slab, o_slab = refs[8:]
    step = pl.program_id(0)
    gain = own_columns(gain_all, ids[0], cols, inner)

    @pl.when(step == 0)
    def _():
        gain_grad[...] = jnp.zeros_like(gain_grad)

    size = gate.shape[0]
    at = pl.ds(pl.multiple_of(step * size, size), size)
    stat = jnp.transpose(sums[...])
    scale = lax.rsqrt(stat[:, 0:1] / inner + norm_eps)
    slope = scale * scale * scale * (stat[:, 1:2] / inner)
    z = gate[...]
    sig = sigmoid(z)
    mixed = mixed_in[...]
    gi = mixed * (z * sig)
    dg = d_gated[...]
    scaled = gi * scale
    gated_c = (scaled * gain).astype(bf16)
    gated[at, :] = gated_c
    gain_grad[...] += jnp.sum(dg * scaled, axis=0, keepdims=True)
    d_gi = scale * (gain * dg) - gi * slope
    d_mixed[...] = d_gi * (z * sig)
    d_gate[at, :] = (d_gi * mixed * (sig * (1.0 + z * (1.0 - sig)))).astype(bf16)
    out_part[...] = dot(gated_c, w_o[...], 1, 0).astype(bf16)

    @pl.when(step == pl.num_programs(0) - 1)
    def _():
        turn_slabs(dims, gated, d_gate, normed, cotan, z_slab, o_slab)


def turn_slabs(dims, gated, d_gate, normed, cotan, z_slab, o_slab):
    cols, _, shards, deep = dims
    first, second = bit_orders(shards)
    rows_slab(normed, d_gate[...], z_slab, None, deep, first, None, 0)
    model = cotan.shape[1]
    strip = cols // 2
    bands = shards * strip // model
    size = max(2 * deep, LANES)
    for g in range(cols // size):
        left = gated[:, g * size : (g + 1) * size]
        for a in range(model // strip):
            part = dot(left, cotan[:, a * strip : (a + 1) * strip], 0, 0).astype(bf16)
            for i in range(size // deep):
                r, t = divmod(g * size // deep + i, 2)
                o_slab[slot(a * bands + r, second), :, t * strip : (t + 1) * strip] = part[
                    i * deep : (i + 1) * deep, :
                ]


def rows_slab(left, right, a_slab, b_slab, deep, first, second, cut):
    size = max(deep, LANES)
    for g in range(left.shape[1] // size):
        part = dot(left[:, g * size : (g + 1) * size], right, 0, 0).astype(bf16)
        for i in range(size // deep):
            owner = g * size // deep + i
            mine = part[i * deep : (i + 1) * deep, :]
            if b_slab is None:
                a_slab[slot(owner, first)] = mine
            else:
                a_slab[slot(owner, first)] = mine[:, :cut]
                b_slab[slot(owner, second)] = mine[:, cut:]


def weight_kernel(dims, normed, d_proj, a_slab, b_slab):
    shards, deep, cut = dims
    first, second = bit_orders(shards)
    rows_slab(normed, d_proj[...], a_slab, b_slab, deep, first, second, cut)


def entry_kernel(d_proj, d_gate, w_one, w_z, normed, gain, after, d_normed, norm_grad):
    step = pl.program_id(0)

    @pl.when(step == 0)
    def _():
        norm_grad[...] = jnp.zeros_like(norm_grad)

    part = dot(d_proj[...], w_one[...], 1, 1) + dot(d_gate[...], w_z[...], 1, 1)
    d_normed[...] = part.astype(bf16)
    norm_grad[...] += jnp.sum(part * normed[...].astype(f32), axis=0, keepdims=True)

    @pl.when(step == pl.num_programs(0) - 1)
    def _():
        norm_grad[...] = norm_grad[...] / gain[...]


def finish_kernel(dims, ids, *refs):
    cols, state, heads, n_seq = dims
    zo, one = refs[:n_seq], refs[n_seq : 2 * n_seq]
    in_grad, out_grad = refs[2 * n_seq :]
    inner = cols * n_seq
    strip = cols // 2
    deep = in_grad.shape[1]
    conv_cols = cols + 2 * state
    shared = None
    steps = None
    for o in range(n_seq):
        q = ids[0] ^ o
        block = pl.ds(pl.multiple_of(q * cols, LANES), cols)
        in_grad[block, :] = jnp.transpose(zo[o][:, :cols].astype(f32))
        block = pl.ds(pl.multiple_of(inner + q * cols, LANES), cols)
        in_grad[block, :] = jnp.transpose(one[o][:, :cols].astype(f32))
        band = one[o][:, cols:conv_cols].astype(f32)
        shared = band if shared is None else shared + band
        turned = pltpu.roll(one[o][:, conv_cols:].astype(f32), q * heads, 1)
        steps = turned if steps is None else steps + turned
        block = pl.ds(pl.multiple_of(q * strip, LANES), strip)
        out_grad[:deep, block] = zo[o][:, cols : cols + strip].astype(f32)
        out_grad[deep:, block] = zo[o][:, cols + strip :].astype(f32)
    in_grad[2 * inner : 2 * inner + 2 * state, :] = jnp.transpose(shared)
    in_grad[2 * inner + 2 * state :, :] = jnp.transpose(steps)[: heads * n_seq, :]


def back_kernel(dims, *refs):
    hd, heads, cols, state, inner = dims
    ids, conv_in, conv_out, dt_raw, scan_out, states, d_mixed, conv_w_all, table, picks = refs[:10]
    d_proj, held, halo, conv_grad, head_grad = refs[-5:]
    conv_cols = cols + 2 * state

    @pl.when(pl.program_id(0) == 0)
    def _():
        for start, carried in zip(refs[10:14], (held, halo, conv_grad, head_grad)):
            carried[...] = start[...]

    conv_w = own_columns(conv_w_all, ids[0], cols, inner)
    width = conv_w.shape[0]
    by_head = own_heads(table, ids[0], heads)
    dt_bias, a_log = by_head[0:1, :], by_head[1:2, :]
    skip = spread(by_head, hd, cols)[2:3, :]
    row = lax.broadcasted_iota(jnp.int32, (CHUNK, CHUNK), 0)
    col = lax.broadcasted_iota(jnp.int32, (CHUNK, CHUNK), 1)
    mask = row >= col
    upper = jnp.where(row <= col, 1.0, 0.0).astype(bf16)
    per = LANES // hd
    chunks = conv_in.shape[0] // CHUNK

    @pl.loop(0, chunks)
    def _(turn):
        c = chunks - 1 - turn
        at = pl.ds(pl.multiple_of(c * CHUNK, CHUNK), CHUNK)
        v = conv_out[at, :]
        sig = sigmoid(v)
        active = v * sig
        raw = dt_raw[at, :]
        step, log_decay, cum, cum_t = decays(raw, dt_bias, a_log)
        step_s = spread(step, hd, cols)
        x = active[:, :cols]
        xd = x * step_s
        xd_b = xd.astype(bf16)
        b_b = active[:, cols : cols + state].astype(bf16)
        c_b = active[:, cols + state :].astype(bf16)
        cross = dot(c_b, b_b, 1, 1)
        dm = d_mixed[at, :]
        dy_b = dm.astype(bf16)
        before_b = states[c]
        later = held[...]
        later_b = later.astype(bf16)
        d_cross = jnp.zeros((CHUNK, CHUNK), f32)
        tiles = []
        for j in range(cols // LANES):
            tile = None
            dm_tile = dm[:, j * LANES : (j + 1) * LANES]
            for i in range(per):
                h = j * per + i
                gap = cum[:, h : h + 1] - cum_t[h : h + 1, :]
                fall = jnp.exp(jnp.where(mask, gap, -1e30))
                kern = (fall * cross).astype(bf16)
                out = dot(kern, dy_b[:, j * LANES : (j + 1) * LANES], 0, 0)
                tile = out if tile is None else jnp.where(col >= i * hd, out, tile)
                own = (col >= i * hd) & (col < (i + 1) * hd)
                dy_h = jnp.where(own, dm_tile, 0.0).astype(bf16)
                d_cross = d_cross + fall * dot(dy_h, xd_b[:, j * LANES : (j + 1) * LANES], 1, 1)
            tiles.append(tile)
        intra = jnp.concatenate(tiles, axis=1) if len(tiles) > 1 else tiles[0]
        d_cross_b = d_cross.astype(bf16)
        grown = spread(jnp.exp(cum), hd, cols)
        dy_g = (dm * grown).astype(bf16)
        tail_s = spread(jnp.exp(cum[CHUNK - 1 : CHUNK, :] - cum), hd, cols)
        xt = (xd * tail_s).astype(bf16)
        d_c = dot(d_cross_b, b_b, 1, 0) + dot(dy_g, before_b, 1, 0)
        d_b = dot(d_cross_b, c_b, 0, 0) + dot(xt, later_b, 1, 0)
        inter = tail_s * dot(b_b, later_b, 1, 1)
        held[...] = decay_rows(cum_t, hd, heads, state) * later + dot(dy_g, c_b, 0, 0)
        d_xd = intra + inter
        carried = xd * inter
        change = (
            dy_b.astype(f32) * scan_out[at, :] - xd_b.astype(f32) * intra - carried
        )
        first_row = lax.broadcasted_iota(jnp.int32, (8, cols), 0)
        sums = jnp.where(
            first_row == 0,
            jnp.sum(dm * x, axis=0, keepdims=True),
            jnp.where(first_row == 1, jnp.sum(carried, axis=0, keepdims=True), 0.0),
        )
        by_head = exact(jnp.concatenate([change, x * d_xd, sums], axis=0), picks[...], 1, 0)
        change_h = by_head[:CHUNK]
        step_h = by_head[CHUNK : 2 * CHUNK]
        skip_h = by_head[2 * CHUNK : 2 * CHUNK + 1]
        carried_h = by_head[2 * CHUNK + 1 : 2 * CHUNK + 2]
        kept = before_b.astype(f32) * later
        lane = lax.broadcasted_iota(jnp.int32, (1, LANES), 1)
        kept_h = jnp.zeros((1, LANES), f32)
        for h in range(heads):
            own = jnp.sum(kept[h * hd : (h + 1) * hd, :], axis=0, keepdims=True)
            kept_h = jnp.where(lane == h, jnp.sum(own, axis=1, keepdims=True), kept_h)
        d_log = (
            exact(upper, change_h, 1, 0)
            + jnp.exp(cum[CHUNK - 1 : CHUNK, :]) * kept_h
            + carried_h
        )
        d_step = step_h - d_log * jnp.exp(a_log)
        d_raw = jnp.where(col < heads, d_step * sigmoid(raw + dt_bias), 0.0)
        head_grad[0:1, :] += jnp.sum(d_raw, axis=0, keepdims=True)
        head_grad[1:2, :] += jnp.sum(d_log * log_decay, axis=0, keepdims=True)
        head_grad[2:3, :] += skip_h
        d_x = step_s * d_xd + skip * dm
        d_active = jnp.concatenate([d_x, d_b, d_c], axis=1)
        d_v = d_active * (sig * (1.0 + v * (1.0 - sig)))
        both = jnp.concatenate([d_v, halo[...]], axis=0)
        halo[...] = d_v[:HALO, :]
        entered = conv_in[at, :].astype(f32)
        d_in = None
        for k in range(width):
            shifted = both[width - 1 - k : width - 1 - k + CHUNK, :]
            term = conv_w[k : k + 1, :] * shifted
            d_in = term if d_in is None else d_in + term
            conv_grad[k : k + 1, :] += jnp.sum(entered * shifted, axis=0, keepdims=True)
        conv_grad[width : width + 1, :] += jnp.sum(d_v, axis=0, keepdims=True)
        d_proj[at, :conv_cols] = d_in.astype(bf16)
        d_proj[at, conv_cols:] = d_raw.astype(bf16)


def shaped(shape, kind):
    return jax.ShapeDtypeStruct(shape, kind)


def body(
    hidden_in,
    norm_gain,
    in_weight,
    conv_weight,
    conv_bias,
    dt_bias,
    a_log,
    skip,
    inner_gain,
    out_weight,
    out_grad,
):
    n_seq = lax.axis_size("seq")
    n_shard = lax.axis_size("shard")
    me = lax.axis_index("seq")
    own = hidden_in[0]
    cotan_own = out_grad[0]
    rows, model = own.shape
    length = rows * n_seq
    inner = inner_gain.shape[0]
    conv_dim = conv_bias.shape[0]
    width = conv_weight.shape[0]
    heads_all = dt_bias.shape[0]
    hd = inner // heads_all
    state = (conv_dim - inner) // 2
    cols = inner // n_seq
    heads = heads_all // n_seq
    deep = in_weight.shape[0]
    conv_cols = cols + 2 * state
    one = conv_cols + LANES
    chunks = length // CHUNK

    def columns(array, start, size):
        return lax.dynamic_slice_in_dim(array, start, size, axis=array.ndim - 1)

    w_dt = columns(in_weight, inner + conv_dim + me * heads, heads)
    slab_one = jnp.concatenate(
        [
            columns(in_weight, inner + me * cols, cols),
            in_weight[:, 2 * inner : 2 * inner + 2 * state],
            jnp.pad(w_dt, ((0, 0), (0, LANES - heads))),
        ],
        axis=1,
    )
    bands = n_shard // n_seq
    strip = model // n_seq
    route = [
        (q * n_shard + s, (s // bands) * n_shard + q * bands + s % bands)
        for s in range(n_shard)
        for q in range(n_seq)
    ]
    out_rows = out_weight.shape[0]
    sent = columns(out_weight, me * strip, strip)
    tile = lax.ppermute(sent, ("seq", "shard"), route)
    slab_two = jnp.concatenate(
        [columns(in_weight, me * cols, cols), tile[:deep], tile[deep:]], axis=1
    )

    tok_blocks = seq_gather(own)
    cut_one = one // LANES // 2 * LANES
    ring_one = RingGather(slab_one, cut_one)
    while ring_one.step():
        pass
    n_bits = n_shard.bit_length() - 1
    late = lax.optimization_barrier((slab_two, cotan_own.astype(bf16), ring_one.a, ring_one.b))
    slab_two, cotan_b, ring_one.found[-2:] = (
        late[0],
        late[1],
        [(late[2], ring_one.found[-2][1], 0), (late[3], ring_one.found[-1][1], cut_one)],
    )
    ring_one = ring_one.found
    cot_blocks = seq_gather(cotan_b)
    ring_two = RingGather(slab_two, cols)

    ids = jnp.stack([me, lax.axis_index("shard")]).astype(jnp.int32)
    table = jnp.pad(
        jnp.stack([dt_bias, a_log, skip]), ((0, 5), (0, LANES - heads_all))
    )
    picks = jnp.where(jnp.arange(cols)[:, None] // hd == jnp.arange(LANES)[None, :], 1.0, 0.0)
    picks = picks.astype(bf16)

    n_one = len(ring_one)
    per_block = rows // CHUNK
    steps = n_seq // FRONT_PIECES
    kept = [
        (shaped((length, model), bf16), (rows, model)),
        (shaped((length, conv_cols), bf16), (rows, conv_cols)),
        (shaped((length, conv_cols), f32), (rows, conv_cols)),
        (shaped((length, LANES), f32), (rows, LANES)),
        (shaped((length, cols), f32), (rows, cols)),
        (shaped((chunks, cols, state), bf16), (per_block, cols, state)),
    ]

    def part(block, first, sign=1):
        return pl.BlockSpec(block, lambda i: (first + sign * i,) + (0,) * (len(block) - 1))

    stream = lambda width: pl.BlockSpec((rows, width), lambda i: (i, 0))

    carry_shapes = [shaped((cols, state), f32), shaped((HALO, conv_cols), f32)]
    front_cost = pl.CostEstimate(
        flops=steps * (2 * rows * model * one + 8 * rows * CHUNK * cols),
        bytes_accessed=steps * 12 * rows * model,
        transcendentals=steps * rows * CHUNK * heads,
    )
    constants = (norm_gain[None], conv_weight, conv_bias[None], table)
    dims = (hd, heads, cols, state, inner, n_seq, n_shard, cut_one)
    tokens, w_one, *rest = pl.pallas_call(
        functools.partial(front_kernel, dims + (None,)),
        name="front_0",
        grid=(steps,),
        in_specs=[SMEM] + [ANY] * (n_seq + n_one) + [VMEM] * 4,
        out_specs=[VMEM] * 2 + [part(block, 0) for _, block in kept] + [VMEM] * 2,
        out_shape=[shaped((length, model), bf16), shaped((model, one), bf16)]
        + [shape for shape, _ in kept]
        + carry_shapes,
        scratch_shapes=[
            pltpu.SemaphoreType.DMA((n_seq + n_one,)),
            pltpu.VMEM((rows, one), f32),
        ],
        cost_estimate=front_cost,
    )(ids, *tok_blocks, *[b for b, _, _ in ring_one], *constants)
    saved, carry = rest[:6], rest[6:]
    hops = -(-(n_shard // 2 - 1) // FRONT_PIECES)
    for j in range(1, FRONT_PIECES):
        arrived = [x for _ in range(hops) for x in ring_two.step()][-2:]
        n_skip = len(arrived) + 6
        *rest, held, halo = pl.pallas_call(
            functools.partial(front_kernel, dims + (n_skip,)),
            grid=(steps,),
            in_specs=[SMEM, part((rows, model), j * steps)] + [VMEM] * 7 + [ANY] * n_skip,
            out_specs=[part(block, j * steps) for _, block in kept] + [VMEM] * 2,
            out_shape=[shape for shape, _ in kept] + carry_shapes,
            input_output_aliases={9 + len(arrived) + i: i for i in range(6)},
            scratch_shapes=[pltpu.VMEM((rows, one), f32)],
            cost_estimate=front_cost,
        )(ids, tokens, w_one, *constants, *carry, *arrived, *saved)
        saved, carry = rest, (held, halo)
    normed, conv_in, conv_out, dt_raw, scan_out, states = saved
    while ring_two.step():
        pass
    ring_two = ring_two.found

    n_two = len(ring_two)
    wide = [shaped((length, cols), f32)] * 3
    cotan, w_z, w_o, gate, mixed, d_gated, sums = pl.pallas_call(
        functools.partial(gate_kernel, (cols, heads, hd, n_seq, n_shard)),
        name="gate",
        grid=(n_seq,),
        in_specs=[SMEM]
        + [ANY] * (n_seq + n_two)
        + [stream(model), stream(cols), stream(cols)]
        + [VMEM] * 2,
        out_specs=[VMEM] * 3
        + [stream(cols)] * 3
        + [pl.BlockSpec((8, rows), lambda i: (0, i))],
        out_shape=[
            shaped((length, model), bf16),
            shaped((model, cols), bf16),
            shaped((cols, model), bf16),
            *wide,
            shaped((8, length), f32),
        ],
        scratch_shapes=[pltpu.SemaphoreType.DMA((n_seq + 3 * n_two,))],
        cost_estimate=pl.CostEstimate(
            flops=4 * length * model * cols,
            bytes_accessed=14 * length * model,
            transcendentals=2 * length * cols,
        ),
    )(
        ids,
        *cot_blocks,
        *[b for b, _, _ in ring_two],
        normed,
        conv_out,
        scan_out,
        table,
        inner_gain[None],
    )

    sums = all_sum(sums, "seq")
    _, d_gate, d_mixed, gain_part, out_part, z_slab, o_slab = pl.pallas_call(
        functools.partial(turn_kernel, (cols, inner, n_shard, deep)),
        name="turn",
        grid=(n_seq,),
        in_specs=[SMEM]
        + [stream(cols)] * 3
        + [pl.BlockSpec((8, rows), lambda i: (0, i))]
        + [VMEM] * 4,
        out_specs=[VMEM, VMEM, stream(cols), VMEM, stream(model), VMEM, VMEM],
        out_shape=[
            shaped((length, cols), bf16),
            shaped((length, cols), bf16),
            shaped((length, cols), f32),
            shaped((1, cols), f32),
            shaped((length, model), bf16),
            shaped((n_shard, deep, cols), bf16),
            shaped((n_shard, deep, cols), bf16),
        ],
        cost_estimate=pl.CostEstimate(
            flops=6 * length * cols * model, bytes_accessed=30 * length * cols, transcendentals=0
        ),
    )(ids, gate, mixed, d_gated, sums, inner_gain[None], normed, cotan, w_o)

    halving = Halving((z_slab, o_slab))
    carry = [jnp.zeros(s, f32) for s in ((cols, state), (HALO, conv_cols), (8, conv_cols), (8, LANES))]
    hops = max(1, n_bits // BACK_PIECES)
    steps = n_seq // BACK_PIECES
    d_proj = None
    for j in reversed(range(BACK_PIECES)):
        arrived = []
        if d_proj is not None:
            for _ in range(hops):
                arrived = halving.step() or arrived
        extra = list(arrived) + ([] if d_proj is None else [d_proj])
        last = (j + 1) * steps - 1
        d_proj, *carry = pl.pallas_call(
            functools.partial(back_kernel, (hd, heads, cols, state, inner)),
            grid=(steps,),
            in_specs=[SMEM]
            + [part(block, last, -1) for _, block in kept[1:]]
            + [part((rows, cols), last, -1)]
            + [VMEM] * 7
            + [ANY] * len(extra),
            out_specs=[part((rows, one), last, -1)] + [VMEM] * 4,
            out_shape=[shaped((length, one), bf16)] + [shaped(c.shape, f32) for c in carry],
            input_output_aliases={} if d_proj is None else {13 + len(extra): 0},
            cost_estimate=pl.CostEstimate(
                flops=steps * 20 * rows * CHUNK * cols,
                bytes_accessed=steps * 14 * rows * model,
                transcendentals=steps * rows * CHUNK * heads,
            ),
        )(
            ids,
            conv_in,
            conv_out,
            dt_raw,
            scan_out,
            states,
            d_mixed,
            conv_weight,
            table,
            picks,
            *carry,
            *extra,
        )
    conv_part, head_part = carry[2:]
    a_slab, b_slab = pl.pallas_call(
        functools.partial(weight_kernel, (n_shard, deep, cut_one)),
        name="weight",
        in_specs=[VMEM] * 2,
        out_specs=[VMEM] * 2,
        out_shape=[
            shaped((n_shard, deep, cut_one), bf16),
            shaped((n_shard, deep, one - cut_one), bf16),
        ],
        cost_estimate=pl.CostEstimate(
            flops=2 * length * model * one, bytes_accessed=6 * length * model, transcendentals=0
        ),
    )(normed, d_proj)
    one_own = Halving((a_slab, b_slab)).finish()
    one_all = seq_gather(jnp.concatenate(one_own, axis=1))

    z_own, o_own = halving.finish()
    o_own = lax.ppermute(o_own, ("seq", "shard"), [(b, a) for a, b in route])
    zo_all = seq_gather(jnp.concatenate([z_own, o_own], axis=1))
    in_weight_grad, out_weight_grad = pl.pallas_call(
        functools.partial(finish_kernel, (cols, state, heads, n_seq)),
        name="finish",
        in_specs=[SMEM] + [VMEM] * (2 * n_seq),
        out_specs=[VMEM] * 2,
        out_shape=[shaped((in_weight.shape[1], deep), f32), shaped((out_rows, model), f32)],
    )(ids, *zo_all, *one_all)
    in_weight_grad = in_weight_grad.T

    block_out = own.astype(f32) + seq_scatter(out_part.reshape(n_seq, rows, model))

    d_normed, norm_part = pl.pallas_call(
        entry_kernel,
        name="entry",
        grid=(n_seq,),
        in_specs=[stream(one), stream(cols), VMEM, VMEM, stream(model), VMEM, ANY],
        out_specs=[stream(model), VMEM],
        out_shape=[shaped((length, model), bf16), shaped((1, model), f32)],
        cost_estimate=pl.CostEstimate(
            flops=3 * length * model * one, bytes_accessed=10 * length * model, transcendentals=0
        ),
    )(d_proj, d_gate, w_one, w_z, normed, norm_gain[None], a_slab)
    d_own = seq_scatter(d_normed.reshape(n_seq, rows, model))
    own_f = own.astype(f32)
    rstat = lax.rsqrt(jnp.mean(own_f * own_f, axis=-1, keepdims=True) + norm_eps)
    scaled = norm_gain * d_own
    along = jnp.mean(scaled * own_f, axis=-1, keepdims=True)
    input_grad = cotan_own + rstat * scaled - own_f * rstat * rstat * rstat * along

    def placed(array, size, start):
        wide = jnp.zeros((array.shape[0], size), f32)
        return lax.dynamic_update_slice_in_dim(wide, array, start, axis=1)

    packed = jnp.concatenate(
        [
            placed(conv_part[:, :cols], inner, me * cols),
            conv_part[:, cols:],
            placed(head_part[:, :heads], LANES, me * heads),
            placed(gain_part, inner, me * cols).reshape(8, -1),
            norm_part.reshape(8, -1),
        ],
        axis=1,
    )
    packed = all_sum(all_sum(packed, "shard"), "seq")
    head_all = packed[:, conv_dim : conv_dim + heads_all]
    gain_at = conv_dim + LANES
    gain_all = packed[:, gain_at : gain_at + inner // 8].reshape(-1)
    norm_all = packed[:, gain_at + inner // 8 :].reshape(-1)
    return (
        block_out[None],
        input_grad[None],
        norm_all,
        in_weight_grad,
        packed[:width, :conv_dim],
        packed[width, :conv_dim],
        head_all[0],
        head_all[1],
        head_all[2],
        gain_all,
        out_weight_grad,
    )


def solution(mesh):
    tokens = P("shard", "seq", None)
    rows = P("shard", None)

    return jax.shard_map(
        body,
        mesh=mesh,
        in_specs=(tokens, P(), rows, P(), P(), P(), P(), P(), P(), rows, tokens),
        out_specs=(tokens, tokens, P(), rows, P(), P(), P(), P(), P(), P(), rows),
        check_vma=False,
    )
```

```python
import functools

import jax
import jax.numpy as jnp
from jax import lax
from jax.experimental import pallas as pl
from jax.experimental.pallas import tpu as pltpu
from jax.sharding import PartitionSpec as P


bf16 = jnp.bfloat16
f32 = jnp.float32
norm_eps = 1e-05
LANES = 128
SEQ = "seq"
SHARD = "shard"
CHUNK = 128
HALO = 8
CONV, HEAD, GAIN, NORM = range(4)
FRONT_PIECES = 4
BACK_PIECES = 2

VMEM = pl.BlockSpec(memory_space=pltpu.VMEM)
SMEM = pl.BlockSpec(memory_space=pltpu.SMEM)
ANY = pl.BlockSpec(memory_space=pl.ANY)


def swap(block, axis, distance):
    n = lax.axis_size(axis)
    return lax.ppermute(block, axis, [(i, i ^ distance) for i in range(n)])


def seq_gather(block):
    n = lax.axis_size(SEQ)
    blocks = {0: block}
    d = n // 2
    while d >= 1:
        for o in list(blocks):
            blocks[o ^ d] = swap(blocks[o], SEQ, d)
        d //= 2
    return [blocks[o] for o in range(n)]


def seq_scatter(parts):
    n = lax.axis_size(SEQ)
    me = lax.axis_index(SEQ)
    d = 1
    while d < n:
        m = parts.shape[0]
        pairs = parts.reshape((m // 2, 2) + parts.shape[1:])
        bit = (me // d) % 2
        keep = lax.dynamic_index_in_dim(pairs, bit, 1, keepdims=False)
        send = lax.dynamic_index_in_dim(pairs, 1 - bit, 1, keepdims=False)
        got = swap(send.astype(bf16), SEQ, d)
        parts = keep.astype(f32) + got.astype(f32)
        d *= 2
        if d < n:
            parts = parts.astype(bf16)
    return parts[0]


def all_sum(block, axis):
    n = lax.axis_size(axis)
    d = 1
    while d < n:
        got = swap(block, axis, d)
        block = block + got
        d *= 2
    return block


def ring_index(place, n):
    place = lax.rem(place + 2 * n, n)
    return jnp.where(place < n // 2, 2 * place, 2 * (n - place) - 1)


def ring_place(shard, n):
    return jnp.where(shard % 2 == 0, shard // 2, n - (shard + 1) // 2)


def ring_routes(n):
    order = list(range(0, n, 2)) + list(range(n - 1, 0, -2))
    ahead = [(order[p], order[(p + 1) % n]) for p in range(n)]
    return ahead, [(b, a) for a, b in ahead]


class RingGather:
    def __init__(self, block, cut):
        n = lax.axis_size(SHARD)
        self.n, self.cut, self.hop = n, cut, 0
        self.ahead, self.back = ring_routes(n)
        self.place = ring_place(lax.axis_index(SHARD), n)
        self.a = self.b = block
        self.found = [(block, lax.axis_index(SHARD), 0)]

    def step(self):
        if self.hop == self.n // 2:
            return []
        self.hop += 1
        k, n = self.hop, self.n
        if k == n // 2:
            self.a = lax.ppermute(self.a[:, : self.cut], SHARD, self.ahead)
            self.b = lax.ppermute(self.b[:, self.cut :], SHARD, self.back)
            owner = ring_index(self.place - k, n)
            self.found += [(self.a, owner, 0), (self.b, owner, self.cut)]
        else:
            self.a = lax.ppermute(self.a, SHARD, self.ahead)
            self.b = lax.ppermute(self.b, SHARD, self.back)
            self.found.append((self.a, ring_index(self.place - k, n), 0))
            self.found.append((self.b, ring_index(self.place + k, n), 0))
        return [self.a, self.b]


def bit_orders(n):
    bits = list(range(n.bit_length() - 1))
    return bits, [bits[1], bits[0]] + bits[2:]


def slot(owner, bits):
    place = 0
    for b in bits:
        place = 2 * place + ((owner >> b) & 1)
    return place


class Halving:
    def __init__(self, halves, rider=None):
        self.halves = list(halves)
        self.slabs = [None] * len(self.halves)
        self.orders = bit_orders(lax.axis_size(SHARD))
        self.hop = 0
        self.rider = rider

    def step(self):
        if self.hop == len(self.orders[0]):
            return []
        me = lax.axis_index(SHARD)
        for i, slab in enumerate(self.slabs):
            b = self.orders[i][self.hop]
            if slab is None:
                keep, send = self.halves[i]
            else:
                pair = slab.reshape((2, slab.shape[0] // 2) + slab.shape[1:])
                bit = (me >> b) & 1
                keep = lax.dynamic_index_in_dim(pair, bit, 0, keepdims=False)
                send = lax.dynamic_index_in_dim(pair, 1 - bit, 0, keepdims=False)
                if i == 0 and self.rider is not None:
                    flat = send.reshape(-1, send.shape[2])
                    send = jnp.concatenate([flat, self.rider], axis=0)
            got = swap(send, SHARD, 1 << b)
            if i == 0 and self.rider is not None:
                rows = keep.shape[0] * keep.shape[1]
                self.rider = two_parts(joined(got[rows:]) + joined(self.rider))
                got = got[:rows].reshape(keep.shape)
            self.slabs[i] = (keep.astype(f32) + got.astype(f32)).astype(bf16)
        self.hop += 1
        return self.slabs

    def finish(self):
        while self.step():
            pass
        return [s[0] for s in self.slabs]


def two_parts(x):
    high = lax.reduce_precision(x, 8, 7)
    return jnp.concatenate([high.astype(bf16), (x - high).astype(bf16)], axis=0)


def joined(parts):
    n = parts.shape[0] // 2
    return parts[:n].astype(f32) + parts[n:].astype(f32)


def put(halves, shard, owner, bits, value, at=slice(None)):
    half = ((shard >> bits[0]) & 1) ^ ((owner >> bits[0]) & 1)
    halves[half, slot(owner, bits[1:]), :, at] = value


def sigmoid(v):
    return 1.0 / (1.0 + jnp.exp(-v))


def softplus(v):
    return jnp.maximum(v, 0.0) + jnp.log1p(jnp.exp(-jnp.abs(v)))


def dot(left, right, l, r, precision=None):
    return lax.dot_general(
        left, right, (((l,), (r,)), ((), ())), preferred_element_type=f32, precision=precision
    )


def exact(left, right, l, r):
    total = None
    whole, ones = (right, left) if left.dtype == bf16 else (left, right)
    for _ in range(3):
        piece = whole.astype(bf16)
        whole = whole - piece.astype(f32)
        pair = (ones, piece) if left.dtype == bf16 else (piece, ones)
        term = dot(*pair, l, r)
        total = term if total is None else total + term
    return total


def spread(per_head, hd, cols):
    rows = per_head.shape[0]
    lane = lax.broadcasted_iota(jnp.int32, (rows, LANES), 1)
    tiles = []
    per = LANES // hd
    for j in range(cols // LANES):
        tile = jnp.broadcast_to(per_head[:, j * per : j * per + 1], (rows, LANES))
        for i in range(1, per):
            h = j * per + i
            tile = jnp.where(
                lane >= i * hd, jnp.broadcast_to(per_head[:, h : h + 1], (rows, LANES)), tile
            )
        tiles.append(tile)
    return jnp.concatenate(tiles, axis=1) if len(tiles) > 1 else tiles[0]


def decay_rows(cum_t, hd, heads, state):
    last = cum_t.shape[1] - 1
    return jnp.concatenate(
        [
            jnp.broadcast_to(jnp.exp(cum_t[h : h + 1, last : last + 1]), (hd, state))
            for h in range(heads)
        ],
        axis=0,
    )


def assemble(copies, sems):
    handles = []
    for i, (src, dst, owner, col) in enumerate(copies):
        rows, cols = src.shape
        place = pl.multiple_of(owner * rows, rows)
        handle = pltpu.make_async_copy(
            src, dst.at[pl.ds(place, rows), col : col + cols], sems.at[i]
        )
        handle.start()
        handles.append(handle)
    for handle in handles:
        handle.wait()


def ring_owners(shard, n, cut):
    place = ring_place(shard, n)
    found = [(shard, 0)]
    for k in range(1, n // 2):
        found.append((ring_index(place - k, n), 0))
        found.append((ring_index(place + k, n), 0))
    last = ring_index(place - n // 2, n)
    return found + [(last, 0), (last, cut)]


def own_heads(table, me, heads):
    return pltpu.roll(table[...], lax.rem(LANES - me * heads, LANES), 1)


def own_columns(ref, me, cols, inner):
    mine = ref[:, pl.ds(pl.multiple_of(me * cols, LANES), cols)]
    if inner == ref.shape[1]:
        return mine
    return jnp.concatenate([mine, ref[:, inner:]], axis=1)


def decays(dt_raw, dt_bias, a_log):
    rows = dt_raw.shape[0]
    row = lax.broadcasted_iota(jnp.int32, (rows, rows), 0)
    col = lax.broadcasted_iota(jnp.int32, (rows, rows), 1)
    lower = jnp.where(row >= col, 1.0, 0.0).astype(bf16)
    step = softplus(dt_raw + dt_bias)
    log_decay = -step * jnp.exp(a_log)
    cum = exact(lower, log_decay, 1, 0)
    cum_t = jnp.transpose(cum)
    return step, log_decay, cum, cum_t


def front_kernel(dims, ids, *refs):
    hd, heads, cols, state, inner, n_seq, n_shard, w_cut, n_skip = dims
    conv_cols = cols + 2 * state
    me = ids[0]
    step = pl.program_id(0)
    if n_skip is None:
        n_w = n_shard + 1
        tok_refs = refs[:n_seq]
        w_refs = refs[n_seq : n_seq + n_w]
        gain, conv_w_all, conv_b_all, table = refs[n_seq + n_w : n_seq + n_w + 4]
        tokens_all, w_all = refs[n_seq + n_w + 4 : n_seq + n_w + 6]
        normed, conv_in, conv_out, dt_raw, scan_out, states, held, halo = refs[-10:-2]
        sems, projected = refs[-2:]

        @pl.when(step == 0)
        def _():
            owners = ring_owners(ids[1], n_shard, w_cut)
            assemble(
                [(r, tokens_all, me ^ o, 0) for o, r in enumerate(tok_refs)]
                + [(r, w_all, o, c) for r, (o, c) in zip(w_refs, owners)],
                sems,
            )
            held[...] = jnp.zeros_like(held)
            halo[...] = jnp.zeros_like(halo)

        size = normed.shape[0]
        tok = tokens_all[pl.ds(pl.multiple_of(step * size, size), size), :].astype(f32)
    else:
        tokens, w_all, gain, conv_w_all, conv_b_all, table, held_in, halo_in = refs[:8]
        normed, conv_in, conv_out, dt_raw, scan_out, states, held, halo, projected = refs[
            8 + n_skip :
        ]

        @pl.when(step == 0)
        def _():
            held[...] = held_in[...]
            halo[...] = halo_in[...]

        tok = tokens[...].astype(f32)
    conv_w = own_columns(conv_w_all, me, cols, inner)
    conv_b = own_columns(conv_b_all, me, cols, inner)
    by_head = own_heads(table, me, heads)
    dt_bias, a_log = by_head[0:1, :], by_head[1:2, :]
    width = conv_w.shape[0]
    row = lax.broadcasted_iota(jnp.int32, (CHUNK, CHUNK), 0)
    col = lax.broadcasted_iota(jnp.int32, (CHUNK, CHUNK), 1)
    mask = row >= col
    per = LANES // hd

    rstat = lax.rsqrt(jnp.mean(tok * tok, axis=1, keepdims=True) + norm_eps)
    nrm = (tok * rstat * gain[...]).astype(bf16)
    normed[...] = nrm
    projected[...] = dot(nrm, w_all[...], 1, 0)

    @pl.loop(0, normed.shape[0] // CHUNK)
    def _(c):
        at = pl.ds(pl.multiple_of(c * CHUNK, CHUNK), CHUNK)
        proj = projected[at, :]
        narrow = proj[:, :conv_cols].astype(bf16)
        conv_in[at, :] = narrow
        wide = narrow.astype(f32)
        both = jnp.concatenate([halo[...], wide], axis=0)
        halo[...] = wide[CHUNK - HALO :, :]
        first = HALO - (width - 1)
        v = conv_b + conv_w[0:1, :] * both[first : first + CHUNK, :]
        for k in range(1, width):
            v = v + conv_w[k : k + 1, :] * both[first + k : first + k + CHUNK, :]
        conv_out[at, :] = v
        active = v * sigmoid(v)
        raw = proj[:, conv_cols:]
        dt_raw[at, :] = raw
        step, _, cum, cum_t = decays(raw, dt_bias, a_log)
        xd = active[:, :cols] * spread(step, hd, cols)
        xd_b = xd.astype(bf16)
        b_b = active[:, cols : cols + state].astype(bf16)
        c_b = active[:, cols + state :].astype(bf16)
        cross = dot(c_b, b_b, 1, 1)
        before = held[...]
        before_b = before.astype(bf16)
        states[c] = before_b
        tiles = []
        for j in range(cols // LANES):
            tile = None
            for i in range(per):
                h = j * per + i
                gap = cum[:, h : h + 1] - cum_t[h : h + 1, :]
                kern = (jnp.exp(jnp.where(mask, gap, -1e30)) * cross).astype(bf16)
                out = dot(kern, xd_b[:, j * LANES : (j + 1) * LANES], 1, 0)
                tile = out if tile is None else jnp.where(col >= i * hd, out, tile)
            tiles.append(tile)
        intra = jnp.concatenate(tiles, axis=1) if len(tiles) > 1 else tiles[0]
        inter = spread(jnp.exp(cum), hd, cols) * dot(c_b, before_b, 1, 1)
        scan_out[at, :] = intra + inter
        tail = jnp.exp(cum[CHUNK - 1 : CHUNK, :] - cum)
        xt = (xd * spread(tail, hd, cols)).astype(bf16)
        held[...] = decay_rows(cum_t, hd, heads, state) * before + dot(xt, b_b, 0, 0)


def gate_kernel(dims, ids, *refs):
    cols, heads, hd, n_seq, n_shard = dims
    n_w = n_shard + 1
    me = ids[0]
    cot_refs = refs[:n_seq]
    w_refs = refs[n_seq : n_seq + n_w]
    normed, conv_out, scan_out, table, gain_all = refs[n_seq + n_w : n_seq + n_w + 5]
    cotan, wz, wo, gate, mixed_out, d_gated, sums, sems = refs[n_seq + n_w + 5 :]
    step = pl.program_id(0)

    @pl.when(step == 0)
    def _():
        copies = [(r, cotan, me ^ o) for o, r in enumerate(cot_refs)]
        assemble_two(copies, w_refs, ring_owners(ids[1], n_shard, cols), wz, wo, sems)

    skip = spread(own_heads(table, me, heads), hd, cols)[2:3, :]
    gain = own_columns(gain_all, me, cols, gain_all.shape[1])
    size = normed.shape[0]
    lane = lax.broadcasted_iota(jnp.int32, (size, LANES), 1)
    z = dot(normed[...], wz[...], 1, 0)
    dg = dot(cotan[pl.ds(pl.multiple_of(step * size, size), size), :], wo[...], 1, 1)
    v = conv_out[...].astype(f32)
    mixed = scan_out[...] + skip * (v * sigmoid(v))
    gi = mixed * (z * sigmoid(z))
    gate[...] = z
    mixed_out[...] = mixed
    d_gated[...] = dg
    squares = jnp.sum(gi * gi, axis=1, keepdims=True)
    slopes = jnp.sum(gi * dg * gain, axis=1, keepdims=True)
    both = jnp.where(lane == 0, squares, jnp.where(lane == 1, slopes, 0.0))
    sums[...] = jnp.transpose(both)[:8, :]


def assemble_two(copies, w_refs, owners, wz, wo, sems):
    rows = w_refs[0].shape[0]
    z_width = wz.shape[1]
    handles = []

    def start(src, dst):
        handle = pltpu.make_async_copy(src, dst, sems.at[len(handles)])
        handle.start()
        handles.append(handle)

    for src, dst, place in copies:
        size = src.shape[0]
        start(src, dst.at[pl.ds(pl.multiple_of(place * size, size), size), :])
    half = z_width // 2
    per = wo.shape[0] // (2 * rows)
    for src, (owner, col) in zip(w_refs, owners):
        if col == 0:
            part = src if src.shape[1] == z_width else src.at[:, 0:z_width]
            start(part, wz.at[pl.ds(pl.multiple_of(owner * rows, rows), rows), :])
        if col + src.shape[1] == 2 * z_width:
            at = 0 if col else z_width
            band = pl.multiple_of(lax.rem(owner, per) * (2 * rows), 2 * rows)
            column = pl.multiple_of(lax.div(owner, per) * half, half)
            for t in range(2):
                start(
                    src.at[:, at + t * half : at + (t + 1) * half],
                    wo.at[pl.ds(band + t * rows, rows), pl.ds(column, half)],
                )
    for handle in handles:
        handle.wait()


def turn_kernel(dims, ids, *refs):
    cols, inner, _, _ = dims
    gate, mixed_in, d_gated, sums, gain_all, normed, cotan, w_o = refs[:8]
    w_z = refs[8]
    gated, d_gate, d_mixed, gain_grad, out_part, norm_z = refs[9:15]
    outs, halves = refs[15:19], refs[19:]
    step = pl.program_id(0)
    gain = own_columns(gain_all, ids[0], cols, inner)

    @pl.when(step == 0)
    def _():
        gain_grad[...] = jnp.zeros_like(gain_grad)

    size = gate.shape[0]
    at = pl.ds(pl.multiple_of(step * size, size), size)
    stat = jnp.transpose(sums[...])
    scale = lax.rsqrt(stat[:, 0:1] / inner + norm_eps)
    slope = scale * scale * scale * (stat[:, 1:2] / inner)
    z = gate[...].astype(f32)
    sig = sigmoid(z)
    mixed = mixed_in[...].astype(f32)
    gi = mixed * (z * sig)
    dg = d_gated[...].astype(f32)
    scaled = gi * scale
    gated_c = (scaled * gain).astype(bf16)
    gated[at, :] = gated_c
    gain_grad[...] += jnp.sum(dg * scaled, axis=0, keepdims=True)
    d_gi = scale * (gain * dg) - gi * slope
    d_mixed[...] = d_gi * (z * sig)
    d_gate[at, :] = (d_gi * mixed * (sig * (1.0 + z * (1.0 - sig)))).astype(bf16)
    out_part[...] = dot(gated_c, w_o[...], 1, 0).astype(bf16)

    @pl.when(step == pl.num_programs(0) - 1)
    def _():
        turn_slabs(dims, ids[1], gated, d_gate, normed, cotan, w_z, norm_z, *halves)
        hand_over(halves, outs)


def turn_slabs(dims, shard, gated, d_gate, normed, cotan, w_z, norm_z, z_halves, o_halves):
    cols, _, shards, deep = dims
    first, second = bit_orders(shards)
    rows_slab(shard, normed, d_gate[...], z_halves, None, deep, first, None, 0, w_z, norm_z)
    model = cotan.shape[1]
    strip = cols // 2
    bands = shards * strip // model
    size = max(2 * deep, LANES)
    for g in range(cols // size):
        left = gated[:, g * size : (g + 1) * size]
        for a in range(model // strip):
            part = dot(left, cotan[:, a * strip : (a + 1) * strip], 0, 0).astype(bf16)
            for i in range(size // deep):
                r, t = divmod(g * size // deep + i, 2)
                value = part[i * deep : (i + 1) * deep, :]
                at = slice(t * strip, (t + 1) * strip)
                put(o_halves, shard, a * bands + r, second, value, at)


def rows_slab(shard, left, right, a_halves, b_halves, deep, first, second, cut, weight, norms):
    size = max(deep, LANES)
    for g in range(left.shape[1] // size):
        at = slice(g * size, (g + 1) * size)
        full = dot(left[:, at], right, 0, 0)
        along = jnp.sum(full * weight[at, :].astype(f32), axis=1, keepdims=True)
        norms[:, at] = jnp.transpose(jnp.broadcast_to(along, (size, LANES)))[:8, :]
        part = full.astype(bf16)
        for i in range(size // deep):
            owner = g * size // deep + i
            mine = part[i * deep : (i + 1) * deep, :]
            if b_halves is None:
                put(a_halves, shard, owner, first, mine)
            else:
                put(a_halves, shard, owner, first, mine[:, :cut])
                put(b_halves, shard, owner, second, mine[:, cut:])


def hand_over(halves, outs):
    for i, half in enumerate(halves):
        outs[2 * i][...] = half[0]
        sent = outs[2 * i + 1]
        if len(sent.shape) == 2:
            rows = half.shape[2]
            for j in range(half.shape[1]):
                sent[j * rows : (j + 1) * rows, :] = half[1, j]
        else:
            sent[...] = half[1]


def small_tiles(width, conv_cols, cols, model):
    found = [(CONV, k, c) for k in range(width + 1) for c in range(0, conv_cols, LANES)]
    found += [(HEAD, k, 0) for k in range(3)]
    found += [(GAIN, 0, c) for c in range(0, cols, LANES)]
    return found + [(NORM, 0, c) for c in range(0, model, LANES)]


def rider_rows(tiles, cut):
    rows = -(-tiles // (cut // LANES))
    return -(-rows // 16) * 16


def weight_kernel(dims, ids, normed, d_proj, w_one, gain, norm_z, conv, head, inner_gain, *refs):
    shards, deep, cut, width = dims
    outs, rider = refs[:4], refs[4]
    halves, norms, packed = refs[5:7], refs[7], refs[8]
    first, second = bit_orders(shards)
    rows_slab(
        ids[1], normed, d_proj[...], *halves, deep, first, second, cut, w_one, norms
    )
    norm = (norms[0:1, :] + norm_z[0:1, :]) / gain[...]
    packed[...] = jnp.zeros_like(packed)
    per = cut // LANES
    kinds = {CONV: conv, HEAD: head, GAIN: inner_gain}
    tiles = small_tiles(width, conv.shape[1], inner_gain.shape[1], normed.shape[1])
    for i, (kind, r, c) in enumerate(tiles):
        tile = norm[:, c : c + LANES] if kind == NORM else kinds[kind][r : r + 1, c : c + LANES]
        at = (i % per) * LANES
        packed[i // per : i // per + 1, at : at + LANES] = tile
    high = packed[...].astype(bf16)
    n = high.shape[0]
    rider[:n, :] = high
    rider[n:, :] = (packed[...] - high.astype(f32)).astype(bf16)
    hand_over(halves, outs)
    sent = outs[1]
    sent[sent.shape[0] - rider.shape[0] :, :] = rider[...]


def entry_kernel(d_proj, d_gate, w_one, w_z, after, d_normed):
    part = dot(d_proj[...], w_one[...], 1, 1) + dot(d_gate[...], w_z[...], 1, 1)
    d_normed[...] = part.astype(bf16)


def finish_kernel(dims, ids, *refs):
    cols, state, heads, n_seq, cut, width = dims
    zo, one = refs[:n_seq], refs[n_seq : 2 * n_seq]
    in_grad, out_grad, conv_w, conv_b, dt_bias, a_log, skip, gain, norm = refs[2 * n_seq :]
    inner = cols * n_seq
    strip = cols // 2
    deep = in_grad.shape[1]
    conv_cols = cols + 2 * state
    shared = None
    steps = None
    for o in range(n_seq):
        q = ids[0] ^ o
        block = pl.ds(pl.multiple_of(q * cols, LANES), cols)
        in_grad[block, :] = jnp.transpose(zo[o][:, :cols].astype(f32))
        block = pl.ds(pl.multiple_of(inner + q * cols, LANES), cols)
        in_grad[block, :] = jnp.transpose(one[o][:deep, :cols].astype(f32))
        band = one[o][:deep, cols:conv_cols].astype(f32)
        shared = band if shared is None else shared + band
        turned = pltpu.roll(one[o][:deep, conv_cols:].astype(f32), q * heads, 1)
        steps = turned if steps is None else steps + turned
        block = pl.ds(pl.multiple_of(q * strip, LANES), strip)
        out_grad[:deep, block] = zo[o][:, cols : cols + strip].astype(f32)
        out_grad[deep:, block] = zo[o][:, cols + strip :].astype(f32)
    in_grad[2 * inner : 2 * inner + 2 * state, :] = jnp.transpose(shared)
    in_grad[2 * inner + 2 * state :, :] = jnp.transpose(steps)[: heads * n_seq, :]
    riders = [joined(ref[deep:, :cut]) for ref in one]
    per = cut // LANES
    table = {HEAD: (dt_bias, a_log, skip)}
    for i, (kind, r, c) in enumerate(small_tiles(width, conv_cols, cols, norm.shape[1])):
        row, at = i // per, (i % per) * LANES
        pieces = [x[row : row + 1, at : at + LANES] for x in riders]
        if kind == NORM:
            norm[:, c : c + LANES] = sum(pieces)
        elif kind == HEAD:
            rolled = [
                pltpu.roll(jnp.broadcast_to(x, (8, LANES)), (ids[0] ^ o) * heads, 1)
                for o, x in enumerate(pieces)
            ]
            table[kind][r][...] = sum(rolled)[0:1, : heads * n_seq]
        elif kind == CONV and c >= cols:
            place = slice(inner + c - cols, inner + c - cols + LANES)
            if r < width:
                conv_w[r : r + 1, place] = sum(pieces)
            else:
                conv_b[:, place] = sum(pieces)
        else:
            for o, x in enumerate(pieces):
                place = pl.ds(pl.multiple_of((ids[0] ^ o) * cols + c, LANES), LANES)
                if kind == GAIN:
                    gain[:, place] = x
                elif r < width:
                    conv_w[r : r + 1, place] = x
                else:
                    conv_b[:, place] = x


def back_kernel(dims, *refs):
    hd, heads, cols, state, inner, fresh = dims
    ids, conv_in, conv_out, dt_raw, scan_out, states, d_mixed, conv_w_all, table = refs[:9]
    d_proj, held, halo, conv_grad, head_grad = refs[-5:]
    conv_cols = cols + 2 * state

    @pl.when(pl.program_id(0) == 0)
    def _():
        for i, carried in enumerate((held, halo, conv_grad, head_grad)):
            carried[...] = jnp.zeros_like(carried) if fresh else refs[9 + i][...]

    conv_w = own_columns(conv_w_all, ids[0], cols, inner)
    width = conv_w.shape[0]
    by_head = own_heads(table, ids[0], heads)
    dt_bias, a_log = by_head[0:1, :], by_head[1:2, :]
    skip = spread(by_head, hd, cols)[2:3, :]
    row = lax.broadcasted_iota(jnp.int32, (CHUNK, CHUNK), 0)
    col = lax.broadcasted_iota(jnp.int32, (CHUNK, CHUNK), 1)
    mask = row >= col
    upper = jnp.where(row <= col, 1.0, 0.0).astype(bf16)
    per = LANES // hd
    chunks = conv_in.shape[0] // CHUNK
    channel = lax.broadcasted_iota(jnp.int32, (cols, LANES), 0)
    head = lax.broadcasted_iota(jnp.int32, (cols, LANES), 1)
    mine = (channel >= head * hd) & (channel < (head + 1) * hd)
    picks = jnp.where(mine, 1.0, 0.0).astype(bf16)

    @pl.loop(0, chunks)
    def _(turn):
        c = chunks - 1 - turn
        at = pl.ds(pl.multiple_of(c * CHUNK, CHUNK), CHUNK)
        v = conv_out[at, :].astype(f32)
        sig = sigmoid(v)
        active = v * sig
        raw = dt_raw[at, :]
        step, log_decay, cum, cum_t = decays(raw, dt_bias, a_log)
        step_s = spread(step, hd, cols)
        x = active[:, :cols]
        xd = x * step_s
        xd_b = xd.astype(bf16)
        b_b = active[:, cols : cols + state].astype(bf16)
        c_b = active[:, cols + state :].astype(bf16)
        cross = dot(c_b, b_b, 1, 1)
        dm = d_mixed[at, :]
        dy_b = dm.astype(bf16)
        before_b = states[c]
        later = held[...]
        later_b = later.astype(bf16)
        d_cross = jnp.zeros((CHUNK, CHUNK), f32)
        tiles = []
        for j in range(cols // LANES):
            tile = None
            dm_tile = dm[:, j * LANES : (j + 1) * LANES]
            for i in range(per):
                h = j * per + i
                gap = cum[:, h : h + 1] - cum_t[h : h + 1, :]
                fall = jnp.exp(jnp.where(mask, gap, -1e30))
                kern = (fall * cross).astype(bf16)
                out = dot(kern, dy_b[:, j * LANES : (j + 1) * LANES], 0, 0)
                tile = out if tile is None else jnp.where(col >= i * hd, out, tile)
                own = (col >= i * hd) & (col < (i + 1) * hd)
                dy_h = jnp.where(own, dm_tile, 0.0).astype(bf16)
                d_cross = d_cross + fall * dot(dy_h, xd_b[:, j * LANES : (j + 1) * LANES], 1, 1)
            tiles.append(tile)
        intra = jnp.concatenate(tiles, axis=1) if len(tiles) > 1 else tiles[0]
        d_cross_b = d_cross.astype(bf16)
        grown = spread(jnp.exp(cum), hd, cols)
        dy_g = (dm * grown).astype(bf16)
        tail_s = spread(jnp.exp(cum[CHUNK - 1 : CHUNK, :] - cum), hd, cols)
        xt = (xd * tail_s).astype(bf16)
        d_c = dot(d_cross_b, b_b, 1, 0) + dot(dy_g, before_b, 1, 0)
        d_b = dot(d_cross_b, c_b, 0, 0) + dot(xt, later_b, 1, 0)
        inter = tail_s * dot(b_b, later_b, 1, 1)
        held[...] = decay_rows(cum_t, hd, heads, state) * later + dot(dy_g, c_b, 0, 0)
        d_xd = intra + inter
        carried = xd * inter
        change = (
            dy_b.astype(f32) * scan_out[at, :] - xd_b.astype(f32) * intra - carried
        )
        first_row = lax.broadcasted_iota(jnp.int32, (8, cols), 0)
        sums = jnp.where(
            first_row == 0,
            jnp.sum(dm * x, axis=0, keepdims=True),
            jnp.where(first_row == 1, jnp.sum(carried, axis=0, keepdims=True), 0.0),
        )
        by_head = exact(jnp.concatenate([change, x * d_xd, sums], axis=0), picks, 1, 0)
        change_h = by_head[:CHUNK]
        step_h = by_head[CHUNK : 2 * CHUNK]
        skip_h = by_head[2 * CHUNK : 2 * CHUNK + 1]
        carried_h = by_head[2 * CHUNK + 1 : 2 * CHUNK + 2]
        kept = before_b.astype(f32) * later
        lane = lax.broadcasted_iota(jnp.int32, (1, LANES), 1)
        kept_h = jnp.zeros((1, LANES), f32)
        for h in range(heads):
            own = jnp.sum(kept[h * hd : (h + 1) * hd, :], axis=0, keepdims=True)
            kept_h = jnp.where(lane == h, jnp.sum(own, axis=1, keepdims=True), kept_h)
        d_log = (
            exact(upper, change_h, 1, 0)
            + jnp.exp(cum[CHUNK - 1 : CHUNK, :]) * kept_h
            + carried_h
        )
        d_step = step_h - d_log * jnp.exp(a_log)
        d_raw = jnp.where(col < heads, d_step * sigmoid(raw + dt_bias), 0.0)
        head_grad[0:1, :] += jnp.sum(d_raw, axis=0, keepdims=True)
        head_grad[1:2, :] += jnp.sum(d_log * log_decay, axis=0, keepdims=True)
        head_grad[2:3, :] += skip_h
        d_x = step_s * d_xd + skip * dm
        d_active = jnp.concatenate([d_x, d_b, d_c], axis=1)
        d_v = d_active * (sig * (1.0 + v * (1.0 - sig)))
        both = jnp.concatenate([d_v, halo[...]], axis=0)
        halo[...] = d_v[:HALO, :]
        entered = conv_in[at, :].astype(f32)
        d_in = None
        for k in range(width):
            shifted = both[width - 1 - k : width - 1 - k + CHUNK, :]
            term = conv_w[k : k + 1, :] * shifted
            d_in = term if d_in is None else d_in + term
            conv_grad[k : k + 1, :] += jnp.sum(entered * shifted, axis=0, keepdims=True)
        conv_grad[width : width + 1, :] += jnp.sum(d_v, axis=0, keepdims=True)
        d_proj[at, :conv_cols] = d_in.astype(bf16)
        d_proj[at, conv_cols:] = d_raw.astype(bf16)


def shaped(shape, kind):
    return jax.ShapeDtypeStruct(shape, kind)


def body(
    hidden_in,
    norm_gain,
    in_weight,
    conv_weight,
    conv_bias,
    dt_bias,
    a_log,
    skip,
    inner_gain,
    out_weight,
    out_grad,
):
    n_seq = lax.axis_size(SEQ)
    n_shard = lax.axis_size(SHARD)
    me = lax.axis_index(SEQ)
    own = hidden_in[0]
    cotan_own = out_grad[0]
    rows, model = own.shape
    length = rows * n_seq
    inner = inner_gain.shape[0]
    conv_dim = conv_bias.shape[0]
    width = conv_weight.shape[0]
    heads_all = dt_bias.shape[0]
    hd = inner // heads_all
    state = (conv_dim - inner) // 2
    cols = inner // n_seq
    heads = heads_all // n_seq
    deep = in_weight.shape[0]
    conv_cols = cols + 2 * state
    one = conv_cols + LANES
    chunks = length // CHUNK

    def columns(array, start, size):
        return lax.dynamic_slice_in_dim(array, start, size, axis=array.ndim - 1)

    w_dt = columns(in_weight, inner + conv_dim + me * heads, heads)
    slab_one = jnp.concatenate(
        [
            columns(in_weight, inner + me * cols, cols),
            in_weight[:, 2 * inner : 2 * inner + 2 * state],
            jnp.pad(w_dt, ((0, 0), (0, LANES - heads))),
        ],
        axis=1,
    )
    bands = n_shard // n_seq
    strip = model // n_seq
    route = [
        (q * n_shard + s, (s // bands) * n_shard + q * bands + s % bands)
        for s in range(n_shard)
        for q in range(n_seq)
    ]
    out_rows = out_weight.shape[0]
    sent = columns(out_weight, me * strip, strip)
    tile = lax.ppermute(sent, (SEQ, SHARD), route)
    slab_two = jnp.concatenate(
        [columns(in_weight, me * cols, cols), tile[:deep], tile[deep:]], axis=1
    )

    tok_blocks = seq_gather(own)
    cut_one = one // LANES // 2 * LANES
    ring_one = RingGather(slab_one, cut_one)
    while ring_one.step():
        pass
    n_bits = n_shard.bit_length() - 1
    late = lax.optimization_barrier((slab_two, cotan_own.astype(bf16), ring_one.a, ring_one.b))
    slab_two, cotan_b, ring_one.found[-2:] = (
        late[0],
        late[1],
        [(late[2], ring_one.found[-2][1], 0), (late[3], ring_one.found[-1][1], cut_one)],
    )
    ring_one = ring_one.found
    cot_blocks = seq_gather(cotan_b)
    ring_two = RingGather(slab_two, cols)

    ids = jnp.stack([me, lax.axis_index(SHARD)]).astype(jnp.int32)
    table = jnp.pad(
        jnp.stack([dt_bias, a_log, skip]), ((0, 5), (0, LANES - heads_all))
    )
    n_one = len(ring_one)
    per_block = rows // CHUNK
    steps = n_seq // FRONT_PIECES
    kept = [
        (shaped((length, model), bf16), (rows, model)),
        (shaped((length, conv_cols), bf16), (rows, conv_cols)),
        (shaped((length, conv_cols), f32), (rows, conv_cols)),
        (shaped((length, LANES), f32), (rows, LANES)),
        (shaped((length, cols), f32), (rows, cols)),
        (shaped((chunks, cols, state), bf16), (per_block, cols, state)),
    ]

    def part(block, first, sign=1):
        return pl.BlockSpec(block, lambda i: (first + sign * i,) + (0,) * (len(block) - 1))

    stream = lambda width: pl.BlockSpec((rows, width), lambda i: (i, 0))

    carry_shapes = [shaped((cols, state), f32), shaped((HALO, conv_cols), f32)]
    front_cost = pl.CostEstimate(
        flops=steps * (2 * rows * model * one + 8 * rows * CHUNK * cols),
        bytes_accessed=steps * 12 * rows * model,
        transcendentals=steps * rows * CHUNK * heads,
    )
    constants = (norm_gain[None], conv_weight, conv_bias[None], table)
    dims = (hd, heads, cols, state, inner, n_seq, n_shard, cut_one)
    tokens, w_one, *rest = pl.pallas_call(
        functools.partial(front_kernel, dims + (None,)),
        name="f0",
        grid=(steps,),
        in_specs=[SMEM] + [ANY] * (n_seq + n_one) + [VMEM] * 4,
        out_specs=[VMEM] * 2 + [part(block, 0) for _, block in kept] + [VMEM] * 2,
        out_shape=[shaped((length, model), bf16), shaped((model, one), bf16)]
        + [shape for shape, _ in kept]
        + carry_shapes,
        scratch_shapes=[
            pltpu.SemaphoreType.DMA((n_seq + n_one,)),
            pltpu.VMEM((rows, one), f32),
        ],
        cost_estimate=front_cost,
    )(ids, *tok_blocks, *[b for b, _, _ in ring_one], *constants)
    saved, carry = rest[:6], rest[6:]
    hops = -(-(n_shard // 2 - 1) // FRONT_PIECES)
    for j in range(1, FRONT_PIECES):
        arrived = [x for _ in range(hops) for x in ring_two.step()][-2:]
        n_skip = len(arrived) + 6
        *rest, held, halo = pl.pallas_call(
            functools.partial(front_kernel, dims + (n_skip,)),
            grid=(steps,),
            in_specs=[SMEM, part((rows, model), j * steps)] + [VMEM] * 7 + [ANY] * n_skip,
            out_specs=[part(block, j * steps) for _, block in kept] + [VMEM] * 2,
            out_shape=[shape for shape, _ in kept] + carry_shapes,
            input_output_aliases={9 + len(arrived) + i: i for i in range(6)},
            scratch_shapes=[pltpu.VMEM((rows, one), f32)],
            cost_estimate=front_cost,
        )(ids, tokens, w_one, *constants, *carry, *arrived, *saved)
        saved, carry = rest, (held, halo)
    normed, conv_in, conv_out, dt_raw, scan_out, states = saved
    while ring_two.step():
        pass
    ring_two = ring_two.found

    n_two = len(ring_two)
    wide = [shaped((length, cols), f32)] * 3
    cotan, w_z, w_o, gate, mixed, d_gated, sums = pl.pallas_call(
        functools.partial(gate_kernel, (cols, heads, hd, n_seq, n_shard)),
        name="gate",
        grid=(n_seq,),
        in_specs=[SMEM]
        + [ANY] * (n_seq + n_two)
        + [stream(model), stream(cols), stream(cols)]
        + [VMEM] * 2,
        out_specs=[VMEM] * 3
        + [stream(cols)] * 3
        + [pl.BlockSpec((8, rows), lambda i: (0, i))],
        out_shape=[
            shaped((length, model), bf16),
            shaped((model, cols), bf16),
            shaped((cols, model), bf16),
            *wide,
            shaped((8, length), f32),
        ],
        scratch_shapes=[pltpu.SemaphoreType.DMA((n_seq + 3 * n_two,))],
        cost_estimate=pl.CostEstimate(
            flops=4 * length * model * cols,
            bytes_accessed=14 * length * model,
            transcendentals=2 * length * cols,
        ),
    )(
        ids,
        *cot_blocks,
        *[b for b, _, _ in ring_two],
        normed,
        conv_out,
        scan_out,
        table,
        inner_gain[None],
    )

    sums = all_sum(sums, SEQ)
    gated, d_gate, d_mixed, gain_part, out_part, norm_z, *halves = pl.pallas_call(
        functools.partial(turn_kernel, (cols, inner, n_shard, deep)),
        name="turn",
        grid=(n_seq,),
        in_specs=[SMEM]
        + [stream(cols)] * 3
        + [pl.BlockSpec((8, rows), lambda i: (0, i))]
        + [VMEM] * 5,
        out_specs=[VMEM, VMEM, stream(cols), VMEM, stream(model)] + [VMEM] * 5,
        out_shape=[
            shaped((length, cols), bf16),
            shaped((length, cols), bf16),
            shaped((length, cols), f32),
            shaped((1, cols), f32),
            shaped((length, model), bf16),
            shaped((8, model), f32),
        ]
        + [shaped((n_shard // 2, deep, cols), bf16)] * 4,
        scratch_shapes=[pltpu.VMEM((2, n_shard // 2, deep, cols), bf16)] * 2,
        cost_estimate=pl.CostEstimate(
            flops=6 * length * cols * model, bytes_accessed=30 * length * cols, transcendentals=0
        ),
    )(ids, gate, mixed, d_gated, sums, inner_gain[None], normed, cotan, w_o, w_z)

    halving = Halving((halves[:2], halves[2:]))
    carry = []
    carry_shapes += [shaped((8, conv_cols), f32), shaped((8, LANES), f32)]
    hops = max(1, n_bits // BACK_PIECES)
    steps = n_seq // BACK_PIECES
    d_proj = None
    for j in reversed(range(BACK_PIECES)):
        arrived = []
        if d_proj is not None:
            for _ in range(hops):
                arrived = halving.step() or arrived
        extra = list(arrived) + ([] if d_proj is None else [d_proj])
        last = (j + 1) * steps - 1
        d_proj, *carry = pl.pallas_call(
            functools.partial(back_kernel, (hd, heads, cols, state, inner, d_proj is None)),
            grid=(steps,),
            in_specs=[SMEM]
            + [part(block, last, -1) for _, block in kept[1:]]
            + [part((rows, cols), last, -1)]
            + [VMEM] * (2 + len(carry))
            + [ANY] * len(extra),
            out_specs=[part((rows, one), last, -1)] + [VMEM] * 4,
            out_shape=[shaped((length, one), bf16)] + carry_shapes,
            input_output_aliases={} if d_proj is None else {12 + len(extra): 0},
            cost_estimate=pl.CostEstimate(
                flops=steps * 20 * rows * CHUNK * cols,
                bytes_accessed=steps * 14 * rows * model,
                transcendentals=steps * rows * CHUNK * heads,
            ),
        )(
            ids,
            conv_in,
            conv_out,
            dt_raw,
            scan_out,
            states,
            d_mixed,
            conv_weight,
            table,
            *carry,
            *extra,
        )
    conv_part, head_part = carry[2:]
    n_rider = 2 * rider_rows(len(small_tiles(width, conv_cols, cols, model)), cut_one)
    half = n_shard // 2
    *halves, rider = pl.pallas_call(
        functools.partial(weight_kernel, (n_shard, deep, cut_one, width)),
        name="weight",
        in_specs=[SMEM] + [VMEM] * 8,
        out_specs=[VMEM] * 5,
        out_shape=[
            shaped((half, deep, cut_one), bf16),
            shaped((half * deep + n_rider, cut_one), bf16),
            shaped((half, deep, one - cut_one), bf16),
            shaped((half, deep, one - cut_one), bf16),
            shaped((n_rider, cut_one), bf16),
        ],
        scratch_shapes=[
            pltpu.VMEM((2, half, deep, cut_one), bf16),
            pltpu.VMEM((2, half, deep, one - cut_one), bf16),
            pltpu.VMEM((8, model), f32),
            pltpu.VMEM((n_rider // 2, cut_one), f32),
        ],
        cost_estimate=pl.CostEstimate(
            flops=2 * length * model * one, bytes_accessed=6 * length * model, transcendentals=0
        ),
    )(ids, normed, d_proj, w_one, norm_gain[None], norm_z, conv_part, head_part, gain_part)
    grads = Halving((halves[:2], halves[2:]), rider)
    one_own = jnp.concatenate(grads.finish(), axis=1)
    rider = jnp.pad(grads.rider, ((0, 0), (0, one - cut_one)))
    one_all = seq_gather(jnp.concatenate([one_own, rider], axis=0))

    z_own, o_own = halving.finish()
    o_own = lax.ppermute(o_own, (SEQ, SHARD), [(b, a) for a, b in route])
    zo_all = seq_gather(jnp.concatenate([z_own, o_own], axis=1))
    in_weight_grad, out_weight_grad, conv_w_grad, *rows_out = pl.pallas_call(
        functools.partial(finish_kernel, (cols, state, heads, n_seq, cut_one, width)),
        name="finish",
        in_specs=[SMEM] + [VMEM] * (2 * n_seq),
        out_specs=[VMEM] * 9,
        out_shape=[
            shaped((in_weight.shape[1], deep), f32),
            shaped((out_rows, model), f32),
            shaped((width, conv_dim), f32),
            shaped((1, conv_dim), f32),
            *[shaped((1, heads_all), f32)] * 3,
            shaped((1, inner), f32),
            shaped((1, model), f32),
        ],
    )(ids, *zo_all, *one_all)
    in_weight_grad = in_weight_grad.T

    out_sum = seq_scatter(out_part.reshape(n_seq, rows, model))
    block_out = own.astype(f32) + out_sum

    d_normed = pl.pallas_call(
        entry_kernel,
        name="e",
        grid=(n_seq,),
        in_specs=[stream(one), stream(cols), VMEM, VMEM, ANY],
        out_specs=stream(model),
        out_shape=shaped((length, model), bf16),
        cost_estimate=pl.CostEstimate(
            flops=3 * length * model * one, bytes_accessed=10 * length * model, transcendentals=0
        ),
    )(d_proj, d_gate, w_one, w_z, halves[0])
    d_own = seq_scatter(d_normed.reshape(n_seq, rows, model))
    own_f = own.astype(f32)
    rstat = lax.rsqrt(jnp.mean(own_f * own_f, axis=-1, keepdims=True) + norm_eps)
    scaled = norm_gain * d_own
    along = jnp.mean(scaled * own_f, axis=-1, keepdims=True)
    input_grad = cotan_own + rstat * scaled - own_f * rstat * rstat * rstat * along

    conv_b_grad, dt_grad, a_log_grad, skip_grad, gain_grad, norm_grad = (r[0] for r in rows_out)
    return (
        block_out[None],
        input_grad[None],
        norm_grad,
        in_weight_grad,
        conv_w_grad,
        conv_b_grad,
        dt_grad,
        a_log_grad,
        skip_grad,
        gain_grad,
        out_weight_grad,
    )


def solution(mesh):
    tokens = P(SHARD, SEQ, None)
    rows = P(SHARD, None)

    return jax.shard_map(
        body,
        mesh=mesh,
        in_specs=(tokens, P(), rows, P(), P(), P(), P(), P(), P(), rows, tokens),
        out_specs=(tokens, tokens, P(), rows, P(), P(), P(), P(), P(), P(), rows),
        check_vma=False,
    )
```
